32 devices in a mesh: dp: 8 (over y, x, core), tensor: 4 (over z).
Axes of the slice: x: 2, y: 2, z: 4, core: 2. Of those that a mesh axis runs over, the one named last changes fastest.
Arguments:
- layer_input: bfloat16 [8192, 2048], P(('dp', 'tensor')), may hold values from -6 to 6
- output_grad: bfloat16 [8192, 2048], P(('dp', 'tensor')), may hold values from -6 to 6
- segment_ids: int32 [8, 1024], P('dp'), may hold values from 0 to 2, as said below
- norm_gain: float32 [2, 2048], replicated, may hold values from 0.5 to 1.5
- gain_mean: float32 [2, 2048], replicated, may hold values from -64 to 64
- gain_square: float32 [2, 2048], replicated, may hold values from 409.6 to 1638.4
- norm_shift: float32 [2, 2048], replicated, may hold values from -3 to 3
- shift_mean: float32 [2, 2048], replicated, may hold values from -64 to 64
- shift_square: float32 [2, 2048], replicated, may hold values from 409.6 to 1638.4
- qkv_bias: float32 [3, 2048], P(None, 'tensor'), may hold values from -3 to 3
- bias_mean: float32 [3, 2048], P(None, 'tensor'), may hold values from -128 to 128
- bias_square: float32 [3, 2048], P(None, 'tensor'), may hold values from 1638.4 to 6553.6
- qkv_weight: float32 [3, 2048, 2048], P(None, 'dp', 'tensor'), may hold values from -0.125 to 0.125
- qkv_mean: float32 [3, 2048, 2048], P(None, 'dp', 'tensor'), may hold values from -128 to 128
- qkv_square: float32 [3, 2048, 2048], P(None, 'dp', 'tensor'), may hold values from 1638.4 to 6553.6
- proj_weight: float32 [2048, 2048], P('tensor', 'dp'), may hold values from -0.5 to 0.5
- proj_mean: float32 [2048, 2048], P('tensor', 'dp'), may hold values from -24 to 24
- proj_square: float32 [2048, 2048], P('tensor', 'dp'), may hold values from 65.536 to 262.144
- feed_weight: float32 [2, 2048, 5632], P(None, 'dp', 'tensor'), may hold values from -0.125 to 0.125
- feed_mean: float32 [2, 2048, 5632], P(None, 'dp', 'tensor'), may hold values from -20 to 20
- feed_square: float32 [2, 2048, 5632], P(None, 'dp', 'tensor'), may hold values from 49.152 to 196.608
- down_weight: float32 [5632, 2048], P('tensor', 'dp'), may hold values from -0.078125 to 0.078125
- down_mean: float32 [5632, 2048], P('tensor', 'dp'), may hold values from -40 to 40
- down_square: float32 [5632, 2048], P('tensor', 'dp'), may hold values from 204.8 to 819.2
Outputs:
- layer_output: float32 [8192, 2048], P(('dp', 'tensor'))
- input_grad: float32 [8192, 2048], P(('dp', 'tensor'))
- gain_grad: float32 [2, 2048], replicated
- gain_step: float32 [2, 2048], replicated
- gain_newmean: float32 [2, 2048], replicated
- gain_newsquare: float32 [2, 2048], replicated
- shift_grad: float32 [2, 2048], replicated
- shift_step: float32 [2, 2048], replicated
- shift_newmean: float32 [2, 2048], replicated
- shift_newsquare: float32 [2, 2048], replicated
- bias_grad: float32 [3, 2048], P(None, 'tensor')
- bias_step: float32 [3, 2048], P(None, 'tensor')
- bias_newmean: float32 [3, 2048], P(None, 'tensor')
- bias_newsquare: float32 [3, 2048], P(None, 'tensor')
- qkv_grad: float32 [3, 2048, 2048], P(None, 'dp', 'tensor')
- qkv_updated: float32 [3, 2048, 2048], P(None, 'dp', 'tensor')
- qkv_newmean: float32 [3, 2048, 2048], P(None, 'dp', 'tensor')
- qkv_newsquare: float32 [3, 2048, 2048], P(None, 'dp', 'tensor')
- proj_grad: float32 [2048, 2048], P('tensor', 'dp')
- proj_updated: float32 [2048, 2048], P('tensor', 'dp')
- proj_newmean: float32 [2048, 2048], P('tensor', 'dp')
- proj_newsquare: float32 [2048, 2048], P('tensor', 'dp')
- feed_grad: float32 [2, 2048, 5632], P(None, 'dp', 'tensor')
- feed_updated: float32 [2, 2048, 5632], P(None, 'dp', 'tensor')
- feed_newmean: float32 [2, 2048, 5632], P(None, 'dp', 'tensor')
- feed_newsquare: float32 [2, 2048, 5632], P(None, 'dp', 'tensor')
- down_grad: float32 [5632, 2048], P('tensor', 'dp')
- down_updated: float32 [5632, 2048], P('tensor', 'dp')
- down_newmean: float32 [5632, 2048], P('tensor', 'dp')
- down_newsquare: float32 [5632, 2048], P('tensor', 'dp')
The draws below stay inside these ranges and needn't reach their ends.
Inputs may be any that keep to these rules, and one draw needn't show every extreme that they name: `segment_ids`: in each packed sequence of 1024 tokens the segment numbers start at 0 and never fall; a number may be skipped; the last token's number is 2.
All inputs are finite; a program needn't handle non-finite values.
Results may differ from the reference program's by a relative error of at most 0.012.
Values may be sent and summed in bfloat16 or wider, within the bound.
No kernel may reach another device: no remote copies, remote signals or barrier semaphores. Data moves between devices by JAX's collectives and lax.ppermute only.
A program may use at most 256 MiB of HBM per device.

```python
import math
import jax
import jax.numpy as jnp
from jax import lax

D = 2048
HEADS = 32
HEAD = 64
ROT = 16
FF = 5632
LENGTH = 1024
STEP = 10
SEQS = 8
TOKENS = 8192


def draw_segment_ids(key, part):
    cuts = jax.random.randint(key, (SEQS, 2), 1, LENGTH)
    token_index = jnp.arange(LENGTH, dtype=jnp.int32)[None, :]
    first_doc = (token_index >= cuts[:, 0:1]).astype(jnp.int32)
    second_doc = (token_index >= cuts[:, 1:2]).astype(jnp.int32)
    return first_doc + second_doc


def levels(key, extent, split, least, high):
    level = 1.0
    for dim, parts in split:
        heights = jax.random.uniform(jax.random.fold_in(jax.random.fold_in(key, 6), dim), (parts,), jnp.float32, least / len(split), high / len(split))
        level = level * jnp.repeat(jnp.exp(heights), extent[dim] // parts).reshape((-1,) + (1,) * (len(extent) - 1 - dim))
    return level


def scatter_about(key, extent, deviation, reach, split=(), kind=jnp.bfloat16):
    gain = levels(key, extent, split, -0.22, 0.18) if split else 1.0
    values = jax.random.normal(key, extent, jnp.float32) * deviation * gain
    return jnp.minimum(jnp.maximum(values, -reach), reach).astype(kind)


def setup_inputs(seed: int = 0) -> dict:
    seeds = jax.random.split(jax.random.key(seed), 25)
    layer_input = scatter_about(seeds[0], (TOKENS, D), 1.0, 6.0, ((0, 32),))
    output_grad = scatter_about(seeds[1], (TOKENS, D), 1.0, 6.0, ((0, 32),))
    segment_ids = draw_segment_ids(jax.random.fold_in(seeds[24], 71), 0)
    norm_gain = jnp.clip(1.0 + 0.1 * jax.random.normal(seeds[3], (2, D), jnp.float32), 0.5, 1.5)
    gain_mean = scatter_about(seeds[4], (2, D), (0.11 * TOKENS ** 0.5), 64.0, (), jnp.float32)
    gain_square = jnp.clip(jnp.exp(jax.random.uniform(seeds[5], (2, D), jnp.float32, math.log(409.6), math.log(1638.4))), 409.6, 1638.4)
    norm_shift = scatter_about(seeds[6], (2, D), 0.5, 3.0, (), jnp.float32)
    shift_mean = scatter_about(seeds[7], (2, D), (0.11 * TOKENS ** 0.5), 64.0, (), jnp.float32)
    shift_square = jnp.clip(jnp.exp(jax.random.uniform(seeds[8], (2, D), jnp.float32, math.log(409.6), math.log(1638.4))), 409.6, 1638.4)
    qkv_bias = scatter_about(seeds[9], (3, D), 0.5, 3.0, ((1, 4),), jnp.float32)
    bias_mean = scatter_about(seeds[10], (3, D), (0.22 * TOKENS ** 0.5), 128.0, ((1, 4),), jnp.float32)
    bias_square = jnp.clip(jnp.exp(math.log(6553.6) - 1.3862944 * jax.random.uniform(seeds[11], (3, D), jnp.float32) ** levels(seeds[11], (3, D), ((1, 4),), -0.2, 0.2)), 1638.4, 6553.6)
    qkv_weight = scatter_about(seeds[12], (3, D, D), D ** -0.5, 0.125, ((1, 8), (2, 4)), jnp.float32)
    qkv_mean = scatter_about(seeds[13], (3, D, D), (0.22 * TOKENS ** 0.5), 128.0, ((1, 8), (2, 4)), jnp.float32)
    qkv_square = jnp.clip(jnp.exp(math.log(6553.6) - 1.3862944 * jax.random.uniform(seeds[14], (3, D, D), jnp.float32) ** levels(seeds[14], (3, D, D), ((1, 8), (2, 4)), -0.2, 0.2)), 1638.4, 6553.6)
    proj_weight = scatter_about(seeds[15], (D, D), (D // 16) ** -0.5, 0.5, ((0, 4), (1, 8)), jnp.float32)
    proj_mean = scatter_about(seeds[16], (D, D), (0.045 * TOKENS ** 0.5), 24.0, ((0, 4), (1, 8)), jnp.float32)
    proj_square = jnp.clip(jnp.exp(math.log(262.144) - 1.3862944 * jax.random.uniform(seeds[17], (D, D), jnp.float32) ** levels(seeds[17], (D, D), ((0, 4), (1, 8)), -0.2, 0.2)), 65.536, 262.144)
    feed_weight = scatter_about(seeds[18], (2, D, FF), D ** -0.5, 0.125, ((1, 8), (2, 4)), jnp.float32)
    feed_mean = scatter_about(seeds[19], (2, D, FF), (0.04 * TOKENS ** 0.5), 20.0, ((1, 8), (2, 4)), jnp.float32)
    feed_square = jnp.clip(jnp.exp(math.log(196.608) - 1.3862944 * jax.random.uniform(seeds[20], (2, D, FF), jnp.float32) ** levels(seeds[20], (2, D, FF), ((1, 8), (2, 4)), -0.2, 0.2)), 49.152, 196.608)
    down_weight = scatter_about(seeds[21], (FF, D), FF ** -0.5, 0.078125, ((0, 4), (1, 8)), jnp.float32)
    down_mean = scatter_about(seeds[22], (FF, D), (0.08 * TOKENS ** 0.5), 40.0, ((0, 4), (1, 8)), jnp.float32)
    down_square = jnp.clip(jnp.exp(math.log(819.2) - 1.3862944 * jax.random.uniform(seeds[23], (FF, D), jnp.float32) ** levels(seeds[23], (FF, D), ((0, 4), (1, 8)), -0.2, 0.2)), 204.8, 819.2)
    return dict(layer_input=layer_input, output_grad=output_grad, segment_ids=segment_ids, norm_gain=norm_gain, gain_mean=gain_mean, gain_square=gain_square, norm_shift=norm_shift, shift_mean=shift_mean, shift_square=shift_square, qkv_bias=qkv_bias, bias_mean=bias_mean, bias_square=bias_square, qkv_weight=qkv_weight, qkv_mean=qkv_mean, qkv_square=qkv_square, proj_weight=proj_weight, proj_mean=proj_mean, proj_square=proj_square, feed_weight=feed_weight, feed_mean=feed_mean, feed_square=feed_square, down_weight=down_weight, down_mean=down_mean, down_square=down_square)


@jax.custom_vjp
def low(v):
    return lax.optimization_barrier(v.astype(jnp.bfloat16)).astype(jnp.float32)

@jax.custom_vjp
def low_back(v):
    return v

def low_keep(v):
    return (low(v), None)

def low_pass(kept, grad):
    return (grad,)

def back_keep(v):
    return (v, None)

def back_low(kept, grad):
    return (low(grad),)
low.defvjp(low_keep, low_pass)
low_back.defvjp(back_keep, back_low)
norm_eps = 1e-05
exact_mode = lax.Precision.HIGHEST

def matmul(left, right):
    return jnp.dot(left, right, preferred_element_type=jnp.float32, precision=exact_mode)

def layer_norm(values, gain_row, shift_row):
    center = values - lax.optimization_barrier(jnp.mean(values, axis=-1, keepdims=True))
    spread = lax.optimization_barrier(jnp.mean(center * center, axis=-1, keepdims=True))
    return center * lax.rsqrt(spread + norm_eps) * gain_row + shift_row

def token_positions(segments):
    token_index = jnp.arange(segments.shape[1], dtype=jnp.int32)[None, :]
    starts = jnp.concatenate([jnp.ones((segments.shape[0], 1), dtype=bool), segments[:, 1:] != segments[:, :-1]], axis=1)
    return token_index - lax.cummax(jnp.where(starts, token_index, 0), axis=1)

def rotary_tables(segments):
    half_rot = ROT // 2
    freqs = jnp.exp(jnp.arange(half_rot, dtype=jnp.float32) * (-2.0 * math.log(10000.0) / ROT))
    angles = token_positions(segments).astype(jnp.float32)[:, :, None] * freqs
    angles = jnp.concatenate([angles, angles], axis=-1)
    return (jnp.cos(angles), jnp.sin(angles))

def rotate(values, cosine, sine):
    half_rot = ROT // 2
    rotated_part = values[..., :ROT]
    turned = jnp.concatenate([-rotated_part[..., half_rot:], rotated_part[..., :half_rot]], axis=-1)
    result = rotated_part * cosine[:, :, None, :] + turned * sine[:, :, None, :]
    return jnp.concatenate([result, values[..., ROT:]], axis=-1)

def attention(query, keys, values, segments):
    token_index = jnp.arange(LENGTH, dtype=jnp.int32)
    allowed = (segments[:, :, None] == segments[:, None, :]) & (token_index[:, None] >= token_index[None, :])[None]
    score_scale = HEAD ** (-0.5)

    def one_head(packed):
        q_head, k_head, v_head = packed
        scores = low_back(jnp.einsum('sqd,skd->sqk', q_head, k_head, precision=exact_mode) * score_scale)
        masked = jnp.where(allowed, scores, -1000000000.0)
        row_max = lax.optimization_barrier(jnp.max(masked, axis=-1, keepdims=True))
        exp_terms = jnp.exp(masked - row_max)
        weights = exp_terms / lax.optimization_barrier(jnp.sum(exp_terms, axis=-1, keepdims=True))
        return jnp.einsum('sqk,skd->sqd', low(weights), v_head, precision=exact_mode)
    heads_first = (jnp.moveaxis(query, 2, 0), jnp.moveaxis(keys, 2, 0), jnp.moveaxis(values, 2, 0))
    return jnp.moveaxis(lax.map(jax.checkpoint(one_head), heads_first), 0, 2)

def forward(layer_in, gains, shifts, biases, w_qkv, w_proj, w_feed, w_down, segments):
    seq_count = segments.shape[0]
    normed_one = low(layer_norm(layer_in, gains[0], shifts[0]))
    projected = [low_back(matmul(normed_one, low(w_qkv[which])) + biases[which]) for which in range(3)]
    cosine, sine = rotary_tables(segments)

    def to_heads(values):
        return values.reshape(seq_count, LENGTH, HEADS, HEAD)
    query = low(rotate(to_heads(projected[0]), cosine, sine))
    keys = low(rotate(to_heads(projected[1]), cosine, sine))
    values = low(to_heads(projected[2]))
    mixed = attention(query, keys, values, segments).reshape(seq_count * LENGTH, D)
    mixed = low_back(low(mixed))
    middle = layer_in + low_back(matmul(mixed, low(w_proj)))
    normed_two = low(layer_norm(middle, gains[1], shifts[1]))
    gate = low_back(matmul(normed_two, low(w_feed[0])))
    upper = low_back(matmul(normed_two, low(w_feed[1])))
    hidden = low(jax.nn.silu(gate) * upper)
    return middle + low_back(matmul(hidden, low(w_down)))

def adamw(param, grad_in, mean_in, square_in):
    mean_new = 0.9 * mean_in + 0.1 * grad_in
    square_new = 0.95 * square_in + 0.05 * grad_in * grad_in
    corrected = mean_new / (1.0 - 0.9 ** STEP)
    scaled = jnp.sqrt(square_new / (1.0 - 0.95 ** STEP)) + 1e-08
    change = -0.02 * (corrected / scaled + 0.1 * param)
    return (change, mean_new, square_new)

def reference(layer_input, output_grad, segment_ids, norm_gain, gain_mean, gain_square, norm_shift, shift_mean, shift_square, qkv_bias, bias_mean, bias_square, qkv_weight, qkv_mean, qkv_square, proj_weight, proj_mean, proj_square, feed_weight, feed_mean, feed_square, down_weight, down_mean, down_square):
    group_size = math.gcd(SEQS, 4)
    group_count = SEQS // group_size
    inputs = layer_input.astype(jnp.float32).reshape(group_count, group_size * LENGTH, D)
    cotangent = output_grad.astype(jnp.float32).reshape(group_count, group_size * LENGTH, D)
    segments = segment_ids.reshape(group_count, group_size, LENGTH)
    params = (norm_gain, norm_shift, qkv_bias, qkv_weight, proj_weight, feed_weight, down_weight)

    def one_group(totals, packed):
        layer_in, grad_out, group_segments = packed

        def apply_layer(layer_value, *weights):
            return forward(layer_value, *weights, group_segments)
        result, pullback = jax.vjp(apply_layer, layer_in, *params)
        grads = pullback(grad_out)
        totals = tuple((total + grad_one for total, grad_one in zip(totals, grads[1:])))
        return (totals, (result, grads[0]))
    zero_grads = tuple((jnp.zeros_like(param_arr) for param_arr in params))
    totals, (results, input_grads) = lax.scan(one_group, zero_grads, (inputs, cotangent, segments))
    layer_output = results.reshape(TOKENS, D)
    input_grad = input_grads.reshape(TOKENS, D)
    moments = ((gain_mean, gain_square), (shift_mean, shift_square), (bias_mean, bias_square), (qkv_mean, qkv_square), (proj_mean, proj_square), (feed_mean, feed_square), (down_mean, down_square))
    outputs = [layer_output, input_grad]
    for which, (param_arr, grad_total, pair) in enumerate(zip(params, totals, moments)):
        change, mean_new, square_new = adamw(param_arr, grad_total, pair[0], pair[1])
        shown = change if which < 3 else param_arr + change
        outputs.extend([grad_total, shown, mean_new, square_new])
    return tuple(outputs)
```

```python
import functools
import math

import jax
import jax.numpy as jnp
from jax import lax
from jax.experimental import pallas as pl
from jax.experimental.pallas import tpu as pltpu
from jax.sharding import PartitionSpec as P

HEAD = 64
ROT = 16
HALF = ROT // 2
STEP = 10
PAIR = 2
MASKED = -1000000000.0
BF16 = jnp.bfloat16
F32 = jnp.float32

norm_eps = 1e-05


def norm_forward(values, gain_row, shift_row):
    center = values - jnp.mean(values, axis=-1, keepdims=True)
    inverse = lax.rsqrt(jnp.mean(center * center, axis=-1, keepdims=True) + norm_eps)
    unit_rows = center * inverse
    return (unit_rows * gain_row + shift_row, unit_rows, inverse)


def norm_backward(grad_in, unit_rows, inverse, gain_row):
    scaled = grad_in * gain_row
    return inverse * (
        scaled
        - jnp.mean(scaled, axis=-1, keepdims=True)
        - unit_rows * jnp.mean(scaled * unit_rows, axis=-1, keepdims=True)
    )


def run_starts(segments):
    token_index = jnp.arange(segments.shape[1], dtype=jnp.int32)[None, :]
    starts = jnp.concatenate(
        [jnp.ones((1, 1), dtype=bool), segments[:, 1:] != segments[:, :-1]], axis=1
    )
    return lax.cummax(jnp.where(starts, token_index, 0), axis=1)


def rotary_tables(starts):
    token_index = jnp.arange(starts.shape[1], dtype=jnp.int32)[None, :]
    freqs = jnp.exp(jnp.arange(HALF, dtype=F32) * (-2.0 * math.log(10000.0) / ROT))
    angles = (token_index - starts).astype(F32) * freqs[:, None]
    return (jnp.cos(angles), jnp.sin(angles))


def adamw(param, grad_in, mean_in, square_in):
    mean_new = 0.9 * mean_in + 0.1 * grad_in
    square_new = 0.95 * square_in + 0.05 * grad_in * grad_in
    corrected = mean_new / (1.0 - 0.9**STEP)
    scaled = jnp.sqrt(square_new / (1.0 - 0.95**STEP)) + 1e-08
    change = -0.02 * (corrected / scaled + 0.1 * param)
    return (change, mean_new, square_new)


def contract(left, right, left_dim, right_dim):
    return lax.dot_general(
        left, right, (((left_dim,), (right_dim,)), ((), ())), preferred_element_type=F32
    )


def rope_kernel(where_ref, pre_ref, cos_ref, sin_ref, old_ref, out_ref):
    del where_ref, old_ref
    cosine, sine = cos_ref[...], sin_ref[...]
    for head in range(PAIR):
        rows = slice(head * HEAD, (head + 1) * HEAD)
        for which, factor in ((0, HEAD**-0.5), (1, 1.0)):
            part = pre_ref[which, rows, :]
            first, second = part[:HALF], part[HALF:ROT]
            turned = jnp.concatenate(
                [
                    first * cosine - second * sine,
                    second * cosine + first * sine,
                    part[ROT:],
                ],
                axis=0,
            )
            if factor != 1.0:
                turned = turned * factor
            out_ref[which, rows, :] = turned.astype(BF16)
        out_ref[2, rows, :] = pre_ref[2, rows, :].astype(BF16)


def rope_block(where, pre, cosine, sine, buffer, width, length, block):
    rows = PAIR * HEAD
    first = buffer is None
    body = rope_kernel
    specs = [
        pl.BlockSpec((3, rows, block), lambda h, s: (0, h, 0)),
        pl.BlockSpec((HALF, block), lambda h, s: (0, s[0])),
        pl.BlockSpec((HALF, block), lambda h, s: (0, s[0])),
    ]
    args = [where, pre, cosine, sine]
    aliases = {}
    if first:
        body = lambda a, b, c, d, o: rope_kernel(a, b, c, d, None, o)
    else:
        specs.append(pl.BlockSpec(memory_space=pl.ANY))
        args.append(buffer)
        aliases = {4: 0}
    return pl.pallas_call(
        body,
        out_shape=jax.ShapeDtypeStruct((3, width, length), BF16),
        grid_spec=pltpu.PrefetchScalarGridSpec(
            num_scalar_prefetch=1,
            grid=(width // rows,),
            in_specs=specs,
            out_specs=pl.BlockSpec((3, rows, block), lambda h, s: (0, h, s[0])),
        ),
        input_output_aliases=aliases,
        cost_estimate=pl.CostEstimate(
            flops=6 * 3 * width * block, bytes_accessed=18 * width * block, transcendentals=0
        ),
        name="rope_block",
    )(*args)


def allowed(key_block, query_block, block, starts):
    shape = (block, block)
    key_at = lax.broadcasted_iota(jnp.int32, shape, 0) + key_block * block
    mask = key_at >= starts
    if key_block == query_block:
        query_at = lax.broadcasted_iota(jnp.int32, shape, 1) + query_block * block
        mask = mask & (key_at <= query_at)
    return mask


def attend_kernel(blocks, block, where_ref, starts_ref, q_ref, k_ref, v_ref, out_ref, total_ref):
    starts = starts_ref[...]
    for mine in range(blocks):

        @pl.when(where_ref[0] == mine)
        def _(mine=mine):
            for head in range(PAIR):
                rows = slice(head * HEAD, (head + 1) * HEAD)
                query = q_ref[0, rows, :]
                scores = []
                for other in range(mine + 1):
                    keys = k_ref[0, rows, other * block : (other + 1) * block]
                    raw = contract(keys, query, 0, 0)
                    scores.append(jnp.where(allowed(other, mine, block, starts), raw, MASKED))
                top = functools.reduce(
                    jnp.maximum, [jnp.max(s, axis=0, keepdims=True) for s in scores]
                )
                total = jnp.zeros((1, block), F32)
                result = jnp.zeros((HEAD, block), F32)
                for other, s in enumerate(scores):
                    terms = jnp.exp(s - top)
                    total = total + jnp.sum(terms, axis=0, keepdims=True)
                    values = v_ref[0, rows, other * block : (other + 1) * block]
                    result = result + contract(values, terms.astype(BF16), 1, 0)
                out_ref[rows, :] = (result / total).astype(BF16)
                total_ref[head] = top + jnp.log(total)


def attend_block(where, starts, buffer, block):
    _, width, length = buffer.shape
    rows = PAIR * HEAD
    heads, blocks = width // HEAD, length // block
    return pl.pallas_call(
        functools.partial(attend_kernel, blocks, block),
        out_shape=(
            jax.ShapeDtypeStruct((width, block), BF16),
            jax.ShapeDtypeStruct((heads, 1, block), F32),
        ),
        grid_spec=pltpu.PrefetchScalarGridSpec(
            num_scalar_prefetch=1,
            grid=(width // rows,),
            in_specs=[
                pl.BlockSpec((1, block), lambda h, s: (0, s[0])),
                pl.BlockSpec((1, rows, block), lambda h, s: (0, h, s[0])),
                pl.BlockSpec((1, rows, length), lambda h, s: (1, h, 0)),
                pl.BlockSpec((1, rows, length), lambda h, s: (2, h, 0)),
            ],
            out_specs=(
                pl.BlockSpec((rows, block), lambda h, s: (h, 0)),
                pl.BlockSpec((PAIR, 1, block), lambda h, s: (h, 0, 0)),
            ),
        ),
        cost_estimate=pl.CostEstimate(
            flops=16 * width * block * length,
            bytes_accessed=2 * width * (2 * length + 2 * block),
            transcendentals=heads * block * length,
        ),
        name="attend_block",
    )(where, starts, buffer, buffer, buffer)


def attend_back_kernel(blocks, block, first, last, where_ref, starts_ref, cos_ref, sin_ref, *refs):
    if last:
        all_cos_ref, all_sin_ref, *refs = refs
    q_ref, k_ref, v_ref, grad_ref, total_ref, *refs = refs
    if not first:
        old_ref, *refs = refs
    out_ref, sums_ref = refs
    starts = starts_ref[...]
    cosine, sine = cos_ref[...], sin_ref[...]

    def unrotate(part, cosine, sine):
        one, two = part[:HALF], part[HALF:ROT]
        return jnp.concatenate(
            [one * cosine + two * sine, two * cosine - one * sine, part[ROT:]], axis=0
        )

    for mine in range(blocks):

        @pl.when(where_ref[0] == mine)
        def _(mine=mine):
            for head in range(PAIR):
                rows = slice(head * HEAD, (head + 1) * HEAD)
                query = q_ref[0, rows, :]
                grad = grad_ref[rows, :]
                row_total = total_ref[head]
                kept = []
                offset = jnp.zeros((1, block), F32)
                for other in range(mine + 1):
                    columns = slice(other * block, (other + 1) * block)
                    raw = contract(k_ref[0, rows, columns], query, 0, 0)
                    masked = jnp.where(allowed(other, mine, block, starts), raw, MASKED)
                    weights = jnp.exp(masked - row_total)
                    back = contract(v_ref[0, rows, columns], grad, 0, 0)
                    offset = offset + jnp.sum(weights * back, axis=0, keepdims=True)
                    kept.append((weights, back))
                query_sum = jnp.zeros((HEAD, block), F32)
                for other in range(blocks):
                    columns = slice(other * block, (other + 1) * block)
                    if other <= mine:
                        weights, back = kept[other]
                        change = (weights * (back - offset)).astype(BF16)
                        query_sum = query_sum + contract(k_ref[0, rows, columns], change, 1, 0)
                        key_sum = contract(query, change, 1, 1)
                        value_sum = contract(grad, weights.astype(BF16), 1, 1)
                        if not first:
                            key_sum = key_sum + old_ref[0, rows, columns]
                            value_sum = value_sum + old_ref[1, rows, columns]
                    elif first:
                        key_sum = jnp.zeros((HEAD, block), F32)
                        value_sum = jnp.zeros((HEAD, block), F32)
                    else:
                        key_sum = old_ref[0, rows, columns]
                        value_sum = old_ref[1, rows, columns]
                    if last:
                        at = lax.rem(where_ref[1] + blocks - other, blocks)
                        columns_out = pl.ds(pl.multiple_of(at * block, block), block)
                        turned = unrotate(
                            key_sum, all_cos_ref[:, columns], all_sin_ref[:, columns]
                        )
                        sums_ref[0, rows, columns_out] = turned.astype(BF16)
                        sums_ref[1, rows, columns_out] = value_sum.astype(BF16)
                    else:
                        sums_ref[0, rows, columns] = key_sum
                        sums_ref[1, rows, columns] = value_sum
                query_sum = query_sum * (HEAD**-0.5)
                out_ref[rows, :] = unrotate(query_sum, cosine, sine).astype(BF16)


def attend_back_block(where, starts, cosine, sine, buffer, grad, totals, sums, last):
    _, width, length = buffer.shape
    block = grad.shape[1]
    rows = PAIR * HEAD
    heads, blocks = width // HEAD, length // block
    first = sums is None
    whole_table = pl.BlockSpec((HALF, length), lambda h, s: (0, 0))
    both = pl.BlockSpec((2, rows, length), lambda h, s: (0, h, 0))
    specs = [
        pl.BlockSpec((1, block), lambda h, s: (0, s[0])),
        pl.BlockSpec((HALF, block), lambda h, s: (0, s[0])),
        pl.BlockSpec((HALF, block), lambda h, s: (0, s[0])),
    ]
    args = [starts, cosine, sine]
    if last:
        specs += [whole_table, whole_table]
        args += [cosine, sine]
    specs += [
        pl.BlockSpec((1, rows, block), lambda h, s: (0, h, s[0])),
        pl.BlockSpec((1, rows, length), lambda h, s: (1, h, 0)),
        pl.BlockSpec((1, rows, length), lambda h, s: (2, h, 0)),
        pl.BlockSpec((rows, block), lambda h, s: (h, 0)),
        pl.BlockSpec((PAIR, 1, block), lambda h, s: (h, 0, 0)),
    ]
    args += [buffer, buffer, buffer, grad, totals]
    aliases = {}
    if not first:
        specs.append(both)
        args.append(sums)
        if not last:
            aliases = {len(args): 1}
    return pl.pallas_call(
        functools.partial(attend_back_kernel, blocks, block, first, last),
        out_shape=(
            jax.ShapeDtypeStruct((width, block), BF16),
            jax.ShapeDtypeStruct((2, width, length), BF16 if last else F32),
        ),
        grid_spec=pltpu.PrefetchScalarGridSpec(
            num_scalar_prefetch=1,
            grid=(width // rows,),
            in_specs=specs,
            out_specs=(pl.BlockSpec((rows, block), lambda h, s: (h, 0)), both),
        ),
        input_output_aliases=aliases,
        cost_estimate=pl.CostEstimate(
            flops=40 * width * block * length,
            bytes_accessed=2 * width * (10 * length + 3 * block),
            transcendentals=heads * block * length,
        ),
        name="attend_back_block",
    )(where, *args)


def per_device(
    ring_size,
    data_size,
    layer_input,
    output_grad,
    segment_ids,
    norm_gain,
    gain_mean,
    gain_square,
    norm_shift,
    shift_mean,
    shift_square,
    qkv_bias,
    bias_mean,
    bias_square,
    qkv_weight,
    qkv_mean,
    qkv_square,
    proj_weight,
    proj_mean,
    proj_square,
    feed_weight,
    feed_mean,
    feed_square,
    down_weight,
    down_mean,
    down_square,
):
    n = ring_size
    block, depth = layer_input.shape
    length = n * block
    width = qkv_bias.shape[1]
    place = lax.axis_index("tensor")
    ring = [(i, (i + 1) % n) for i in range(n)]
    barrier = lax.optimization_barrier

    def pass_on(values):
        return lax.ppermute(values, "tensor", ring)

    def ring_gather(values):
        blocks = [values]
        for _ in range(n - 1):
            blocks.append(pass_on(blocks[-1]))
        return blocks

    def ring_scatter(parts):
        moving = None
        for step in range(1, n):
            term = parts[step]
            if moving is not None:
                term = term + moving.astype(F32)
            moving = pass_on(term.astype(BF16))
        return parts[0] + moving.astype(F32)

    def gather_weight(shard, axis):
        return lax.all_gather(shard.astype(BF16), "dp", axis=axis, tiled=True)

    inputs = layer_input.astype(F32)
    w_qkv = gather_weight(qkv_weight, 1)
    w_proj = gather_weight(proj_weight, 1)
    w_feed = gather_weight(feed_weight, 1)
    w_down = gather_weight(down_weight, 1)
    normed_one, unit_one, inverse_one = norm_forward(inputs, norm_gain[0], norm_shift[0])
    rows_one = ring_gather(normed_one.astype(BF16))
    starts = run_starts(segment_ids)
    cosine, sine = rotary_tables(starts)
    wheres = [
        jnp.stack([lax.rem(place + n - p, n), place]).astype(jnp.int32) for p in range(n)
    ]

    buffer = None
    for p in range(n):
        pre = (
            jnp.einsum("kdc,rd->kcr", w_qkv, rows_one[p], preferred_element_type=F32)
            + qkv_bias[:, :, None]
        )
        buffer = rope_block(wheres[p], pre, cosine, sine, buffer, width, length, block)

    mixed, totals, parts = [None] * n, [None] * n, [None] * n
    for p in [*range(1, n), 0]:
        mixed[p], totals[p] = attend_block(wheres[p], starts, buffer, block)
        parts[p] = contract(mixed[p], w_proj, 0, 0)
    middle = inputs + ring_scatter(parts)
    grad_rows = ring_gather(output_grad)

    normed_two, unit_two, inverse_two = norm_forward(middle, norm_gain[1], norm_shift[1])
    rows_two = ring_gather(normed_two.astype(BF16))
    hidden, grad_gate, grad_upper, out_parts, back_parts = [], [], [], [], []
    for p in range(n):
        gate = jnp.dot(rows_two[p], w_feed[0], preferred_element_type=F32)
        upper = jnp.dot(rows_two[p], w_feed[1], preferred_element_type=F32)
        grad_hidden = contract(grad_rows[p], w_down, 1, 1)
        sigma = jax.nn.sigmoid(gate)
        swish = gate * sigma
        hidden.append((swish * upper).astype(BF16))
        grad_gate.append(
            (grad_hidden * upper * sigma * (1.0 + gate * (1.0 - sigma))).astype(BF16)
        )
        grad_upper.append((grad_hidden * swish).astype(BF16))
        back_parts.append(
            contract(grad_gate[p], w_feed[0], 1, 1) + contract(grad_upper[p], w_feed[1], 1, 1)
        )
        out_parts.append(jnp.dot(hidden[p], w_down, preferred_element_type=F32))
    grad_normed_two = ring_scatter(back_parts)
    layer_output = middle + ring_scatter(out_parts)

    grad_middle = output_grad.astype(F32) + norm_backward(
        grad_normed_two, unit_two, inverse_two, norm_gain[1]
    )
    gain_two = jnp.sum(grad_normed_two * unit_two, axis=0)
    shift_two = jnp.sum(grad_normed_two, axis=0)
    rows_back = ring_gather(grad_middle.astype(BF16))

    all_hidden = jnp.concatenate(hidden, axis=0)
    all_rows_two = jnp.concatenate(rows_two, axis=0)
    all_grad_rows = jnp.concatenate(grad_rows, axis=0)
    all_grad_gate = jnp.concatenate(grad_gate, axis=0)
    all_grad_upper = jnp.concatenate(grad_upper, axis=0)

    def scatter_sum(grad, axis):
        return lax.psum_scatter(
            grad.astype(BF16), "dp", scatter_dimension=axis, tiled=True
        ).astype(F32)

    down_sum = scatter_sum(contract(all_hidden, all_grad_rows, 0, 0), 1)
    feed_sum = scatter_sum(
        jnp.stack(
            [
                contract(all_rows_two, all_grad_gate, 0, 0).astype(BF16),
                contract(all_rows_two, all_grad_upper, 0, 0).astype(BF16),
            ]
        ),
        1,
    )

    grad_query, sums = [], None
    for p in range(n):
        grad_mixed = contract(w_proj, rows_back[p], 1, 1).astype(BF16)
        grad_one, sums = attend_back_block(
            wheres[p], starts, cosine, sine, buffer, grad_mixed, totals[p], sums, p == n - 1
        )
        grad_query.append(grad_one)
    grad_pre = jnp.concatenate([jnp.concatenate(grad_query, axis=1)[None], sums], axis=0)
    proj_sum = scatter_sum(
        contract(
            jnp.concatenate(mixed, axis=1), jnp.concatenate(rows_back, axis=0), 1, 0
        ),
        1,
    )
    first_parts = [
        jnp.einsum(
            "kcr,kdc->rd",
            grad_pre[:, :, p * block : (p + 1) * block],
            w_qkv,
            preferred_element_type=F32,
        )
        for p in range(n)
    ]
    grad_normed_one = ring_scatter(first_parts)
    qkv_sum = scatter_sum(
        jnp.einsum(
            "rd,kcr->kdc",
            jnp.concatenate(rows_one, axis=0),
            grad_pre,
            preferred_element_type=F32,
        ),
        1,
    )
    bias_local = jnp.sum(grad_pre.astype(F32), axis=2)
    input_grad = grad_middle + norm_backward(grad_normed_one, unit_one, inverse_one, norm_gain[0])
    gain_one = jnp.sum(grad_normed_one * unit_one, axis=0)
    shift_one = jnp.sum(grad_normed_one, axis=0)

    def sum_over(values, axis, size):
        step = 1
        while step < size:
            values = values + lax.ppermute(values, axis, [(i, i ^ step) for i in range(size)])
            step *= 2
        return values

    bias_grad = sum_over(bias_local, "dp", data_size)
    two = sum_over(sum_over(jnp.stack([gain_two, shift_two]), "dp", data_size), "tensor", n)
    one = sum_over(sum_over(jnp.stack([gain_one, shift_one]), "dp", data_size), "tensor", n)
    gain_total = jnp.stack([one[0], two[0]])
    shift_total = jnp.stack([one[1], two[1]])

    outputs = [layer_output, input_grad]
    groups = (
        (norm_gain, gain_total, gain_mean, gain_square),
        (norm_shift, shift_total, shift_mean, shift_square),
        (qkv_bias, bias_grad, bias_mean, bias_square),
        (qkv_weight, qkv_sum, qkv_mean, qkv_square),
        (proj_weight, proj_sum, proj_mean, proj_square),
        (feed_weight, feed_sum, feed_mean, feed_square),
        (down_weight, down_sum, down_mean, down_square),
    )
    for which, (param_arr, grad_total, mean_in, square_in) in enumerate(groups):
        change, mean_new, square_new = adamw(param_arr, grad_total, mean_in, square_in)
        shown = change if which < 3 else param_arr + change
        outputs.extend([grad_total, shown, mean_new, square_new])
    return tuple(outputs)


def solution(mesh):
    tokens, small, bias = P(("dp", "tensor"), None), P(), P(None, "tensor")
    three, two = P(None, "dp", "tensor"), P("tensor", "dp")
    per_param = [small] * 6 + [bias] * 3 + [three] * 3 + [two] * 3 + [three] * 3 + [two] * 3
    outs = [small] * 8 + [bias] * 4 + [three] * 4 + [two] * 4 + [three] * 4 + [two] * 4
    return jax.shard_map(
        functools.partial(per_device, mesh.shape["tensor"], mesh.shape["dp"]),
        mesh=mesh,
        in_specs=(tokens, tokens, P("dp", None), *per_param),
        out_specs=(tokens, tokens, *outs),
        check_vma=False,
    )
```

```python
import functools
import math

import jax
import jax.numpy as jnp
from jax import lax
from jax.experimental import pallas as pl
from jax.experimental.pallas import tpu as pltpu
from jax.sharding import PartitionSpec as P


HEAD = 64
ROT = 16
HALF = ROT // 2
STEP = 10
PAIR = 2
WIDE = 4
MASKED = -1000000000.0
BF16 = jnp.bfloat16
F32 = jnp.float32

norm_eps = 1e-05


def norm_forward(values, gain_row, shift_row):
    center = values - jnp.mean(values, axis=-1, keepdims=True)
    inverse = lax.rsqrt(jnp.mean(center * center, axis=-1, keepdims=True) + norm_eps)
    unit_rows = center * inverse
    return (unit_rows * gain_row + shift_row, unit_rows, inverse)


def norm_backward(grad_in, unit_rows, inverse, gain_row):
    scaled = grad_in * gain_row
    return inverse * (
        scaled
        - jnp.mean(scaled, axis=-1, keepdims=True)
        - unit_rows * jnp.mean(scaled * unit_rows, axis=-1, keepdims=True)
    )


def run_starts(segments):
    token_index = jnp.arange(segments.shape[1], dtype=jnp.int32)[None, :]
    starts = jnp.concatenate(
        [jnp.ones((1, 1), dtype=bool), segments[:, 1:] != segments[:, :-1]], axis=1
    )
    return lax.cummax(jnp.where(starts, token_index, 0), axis=1)


def rotary_tables(starts):
    token_index = jnp.arange(starts.shape[1], dtype=jnp.int32)[None, :]
    freqs = jnp.exp(jnp.arange(HALF, dtype=F32) * (-2.0 * math.log(10000.0) / ROT))
    angles = (token_index - starts).astype(F32) * freqs[:, None]
    return (jnp.cos(angles), jnp.sin(angles))


def adamw(param, grad_in, mean_in, square_in):
    mean_new = 0.9 * mean_in + 0.1 * grad_in
    square_new = 0.95 * square_in + 0.05 * grad_in * grad_in
    corrected = mean_new / (1.0 - 0.9**STEP)
    scaled = jnp.sqrt(square_new / (1.0 - 0.95**STEP)) + 1e-08
    change = -0.02 * (corrected / scaled + 0.1 * param)
    return (change, mean_new, square_new)


def contract(left, right, left_dim, right_dim):
    return lax.dot_general(
        left, right, (((left_dim,), (right_dim,)), ((), ())), preferred_element_type=F32
    )


def rope_kernel(where_ref, q_ref, k_ref, v_ref, cos_ref, sin_ref, old_ref, out_ref):
    del where_ref, old_ref
    cosine, sine = cos_ref[...], sin_ref[...]
    for which, ref in enumerate((q_ref, k_ref, v_ref)):
        whole = ref[...].T
        for head in range(WIDE):
            rows = slice(head * HEAD, (head + 1) * HEAD)
            part = whole[rows]
            if which < 2:
                first, second = part[:HALF], part[HALF:ROT]
                part = jnp.concatenate(
                    [
                        first * cosine - second * sine,
                        second * cosine + first * sine,
                        part[ROT:],
                    ],
                    axis=0,
                )
            if which == 0:
                part = part * (HEAD**-0.5)
            out_ref[which, rows, :] = part.astype(BF16)


def rope_block(where, pre, cosine, sine, buffer, width, length):
    rows = WIDE * HEAD
    groups = width // rows
    block = pre.shape[0]
    first = buffer is None
    body = rope_kernel
    specs = [
        pl.BlockSpec((block, rows), lambda h, s: (0, h)),
        pl.BlockSpec((block, rows), lambda h, s: (0, groups + h)),
        pl.BlockSpec((block, rows), lambda h, s: (0, 2 * groups + h)),
        pl.BlockSpec((HALF, block), lambda h, s: (0, s[0])),
        pl.BlockSpec((HALF, block), lambda h, s: (0, s[0])),
    ]
    args = [where, pre, pre, pre, cosine, sine]
    aliases = {}
    if first:
        body = lambda w, q, k, v, c, d, o: rope_kernel(w, q, k, v, c, d, None, o)
    else:
        specs.append(pl.BlockSpec(memory_space=pl.ANY))
        aliases = {len(args): 0}
        args.append(buffer)
    return pl.pallas_call(
        body,
        out_shape=jax.ShapeDtypeStruct((3, width, length), BF16),
        grid_spec=pltpu.PrefetchScalarGridSpec(
            num_scalar_prefetch=1,
            grid=(groups,),
            in_specs=specs,
            out_specs=pl.BlockSpec((3, rows, block), lambda h, s: (0, h, s[0])),
        ),
        input_output_aliases=aliases,
        cost_estimate=pl.CostEstimate(
            flops=6 * 3 * width * block, bytes_accessed=18 * width * block, transcendentals=0
        ),
        name="rope_block",
    )(*args)


def allowed(key_block, query_block, block, starts):
    shape = (block, block)
    key_at = lax.broadcasted_iota(jnp.int32, shape, 0) + key_block * block
    mask = key_at >= starts
    if key_block == query_block:
        query_at = lax.broadcasted_iota(jnp.int32, shape, 1) + query_block * block
        mask = mask & (key_at <= query_at)
    return mask


def attend_kernel(blocks, block, where_ref, starts_ref, q_ref, k_ref, v_ref, out_ref, total_ref):
    starts = starts_ref[...]
    for mine in range(blocks):

        @pl.when(where_ref[0] == mine)
        def _(mine=mine):
            for head in range(PAIR):
                rows = slice(head * HEAD, (head + 1) * HEAD)
                query = q_ref[0, rows, :]
                scores = []
                for other in range(mine + 1):
                    keys = k_ref[0, rows, other * block : (other + 1) * block]
                    raw = contract(keys, query, 0, 0)
                    scores.append(jnp.where(allowed(other, mine, block, starts), raw, MASKED))
                top = functools.reduce(
                    jnp.maximum, [jnp.max(s, axis=0, keepdims=True) for s in scores]
                )
                total = jnp.zeros((1, block), F32)
                result = jnp.zeros((HEAD, block), F32)
                for other, s in enumerate(scores):
                    terms = jnp.exp(s - top)
                    total = total + jnp.sum(terms, axis=0, keepdims=True)
                    values = v_ref[0, rows, other * block : (other + 1) * block]
                    result = result + contract(values, terms.astype(BF16), 1, 0)
                out_ref[rows, :] = (result / total).astype(BF16)
                total_ref[head] = top + jnp.log(total)


def attend_block(where, starts, buffer, block):
    _, width, length = buffer.shape
    rows = PAIR * HEAD
    heads, blocks = width // HEAD, length // block
    return pl.pallas_call(
        functools.partial(attend_kernel, blocks, block),
        out_shape=(
            jax.ShapeDtypeStruct((width, block), BF16),
            jax.ShapeDtypeStruct((heads, 1, block), F32),
        ),
        grid_spec=pltpu.PrefetchScalarGridSpec(
            num_scalar_prefetch=1,
            grid=(width // rows,),
            in_specs=[
                pl.BlockSpec((1, block), lambda h, s: (0, s[0])),
                pl.BlockSpec((1, rows, block), lambda h, s: (0, h, s[0])),
                pl.BlockSpec((1, rows, length), lambda h, s: (1, h, 0)),
                pl.BlockSpec((1, rows, length), lambda h, s: (2, h, 0)),
            ],
            out_specs=(
                pl.BlockSpec((rows, block), lambda h, s: (h, 0)),
                pl.BlockSpec((PAIR, 1, block), lambda h, s: (h, 0, 0)),
            ),
        ),
        cost_estimate=pl.CostEstimate(
            flops=16 * width * block * length,
            bytes_accessed=2 * width * (2 * length + 2 * block),
            transcendentals=heads * block * length,
        ),
        name="attend_block",
    )(where, starts, buffer, buffer, buffer)


def attend_back_kernel(blocks, block, first, last, where_ref, starts_ref, cos_ref, sin_ref, *refs):
    if last:
        all_cos_ref, all_sin_ref, *refs = refs
    q_ref, k_ref, v_ref, grad_ref, total_ref, *refs = refs
    if not first:
        old_out_ref, old_ref, *refs = refs
    if last:
        (out_ref,) = refs
    else:
        out_ref, sums_ref = refs
    starts = starts_ref[...]
    cosine, sine = cos_ref[...], sin_ref[...]

    def unrotate(part, cosine, sine):
        one, two = part[:HALF], part[HALF:ROT]
        return jnp.concatenate(
            [one * cosine + two * sine, two * cosine - one * sine, part[ROT:]], axis=0
        )

    def at_position(position):
        return pl.ds(pl.multiple_of(position * block, block), block)

    if last:
        for position in range(blocks):
            columns = slice(position * block, (position + 1) * block)
            out_ref[0, :, columns] = old_out_ref[:, columns]

    for mine in range(blocks):

        @pl.when(where_ref[0] == mine)
        def _(mine=mine):
            for head in range(PAIR):
                rows = slice(head * HEAD, (head + 1) * HEAD)
                query = q_ref[0, rows, :]
                grad = grad_ref[rows, :]
                row_total = total_ref[head]
                kept = []
                offset = jnp.zeros((1, block), F32)
                for other in range(mine + 1):
                    columns = slice(other * block, (other + 1) * block)
                    raw = contract(k_ref[0, rows, columns], query, 0, 0)
                    masked = jnp.where(allowed(other, mine, block, starts), raw, MASKED)
                    weights = jnp.exp(masked - row_total)
                    back = contract(v_ref[0, rows, columns], grad, 0, 0)
                    offset = offset + jnp.sum(weights * back, axis=0, keepdims=True)
                    kept.append((weights, back))
                query_sum = jnp.zeros((HEAD, block), F32)
                for other in range(blocks):
                    columns = slice(other * block, (other + 1) * block)
                    if other <= mine:
                        weights, back = kept[other]
                        change = (weights * (back - offset)).astype(BF16)
                        query_sum = query_sum + contract(k_ref[0, rows, columns], change, 1, 0)
                        key_sum = contract(query, change, 1, 1)
                        value_sum = contract(grad, weights.astype(BF16), 1, 1)
                        if not first:
                            key_sum = key_sum + old_ref[0, rows, columns]
                            value_sum = value_sum + old_ref[1, rows, columns]
                    elif first:
                        key_sum = jnp.zeros((HEAD, block), F32)
                        value_sum = jnp.zeros((HEAD, block), F32)
                    else:
                        key_sum = old_ref[0, rows, columns]
                        value_sum = old_ref[1, rows, columns]
                    if last:
                        there = at_position(lax.rem(where_ref[2] + blocks - other, blocks))
                        turned = unrotate(
                            key_sum, all_cos_ref[:, columns], all_sin_ref[:, columns]
                        )
                        out_ref[1, rows, there] = turned.astype(BF16)
                        out_ref[2, rows, there] = value_sum.astype(BF16)
                    else:
                        sums_ref[0, rows, columns] = key_sum
                        sums_ref[1, rows, columns] = value_sum
                query_sum = unrotate(query_sum * (HEAD**-0.5), cosine, sine).astype(BF16)
                if last:
                    out_ref[0, rows, at_position(where_ref[1])] = query_sum
                else:
                    out_ref[rows, :] = query_sum


def attend_back_block(where, starts, cosine, sine, buffer, grad, totals, before, last):
    _, width, length = buffer.shape
    block = grad.shape[1]
    rows = PAIR * HEAD
    heads, blocks = width // HEAD, length // block
    groups = width // rows
    first = before is None
    whole_table = pl.BlockSpec((HALF, length), lambda h, s: (0, 0))
    both = pl.BlockSpec((2, rows, length), lambda h, s: (0, h, 0))
    specs = [
        pl.BlockSpec((1, block), lambda h, s: (0, s[0])),
        pl.BlockSpec((HALF, block), lambda h, s: (0, s[0])),
        pl.BlockSpec((HALF, block), lambda h, s: (0, s[0])),
    ]
    args = [where, starts, cosine, sine]
    if last:
        specs += [whole_table, whole_table]
        args += [cosine, sine]
    specs += [
        pl.BlockSpec((1, rows, block), lambda h, s: (0, h, s[0])),
        pl.BlockSpec((1, rows, length), lambda h, s: (1, h, 0)),
        pl.BlockSpec((1, rows, length), lambda h, s: (2, h, 0)),
        pl.BlockSpec((rows, block), lambda h, s: (h, 0)),
        pl.BlockSpec((PAIR, 1, block), lambda h, s: (s[1] * groups + h, 0, 0)),
    ]
    args += [buffer, buffer, buffer, grad, totals]
    aliases = {}
    if not first:
        if last:
            specs += [pl.BlockSpec((rows, length), lambda h, s: (h, 0)), both]
        else:
            specs += [pl.BlockSpec(memory_space=pl.ANY), both]
            aliases = {len(args): 0, len(args) + 1: 1}
        args += before
    if last:
        out_shape = jax.ShapeDtypeStruct((3, width, length), BF16)
        out_specs = pl.BlockSpec((3, rows, length), lambda h, s: (0, h, 0))
    else:
        out_shape = (
            jax.ShapeDtypeStruct((width, length), BF16),
            jax.ShapeDtypeStruct((2, width, length), F32),
        )
        out_specs = (pl.BlockSpec((rows, block), lambda h, s: (h, s[1])), both)
    return pl.pallas_call(
        functools.partial(attend_back_kernel, blocks, block, first, last),
        out_shape=out_shape,
        grid_spec=pltpu.PrefetchScalarGridSpec(
            num_scalar_prefetch=1, grid=(groups,), in_specs=specs, out_specs=out_specs
        ),
        input_output_aliases=aliases,
        cost_estimate=pl.CostEstimate(
            flops=40 * width * block * length,
            bytes_accessed=2 * width * (10 * length + 3 * block),
            transcendentals=heads * block * length,
        ),
        name="attend_back_block",
    )(*args)


def per_device(
    ring_size,
    data_size,
    layer_input,
    output_grad,
    segment_ids,
    norm_gain,
    gain_mean,
    gain_square,
    norm_shift,
    shift_mean,
    shift_square,
    qkv_bias,
    bias_mean,
    bias_square,
    qkv_weight,
    qkv_mean,
    qkv_square,
    proj_weight,
    proj_mean,
    proj_square,
    feed_weight,
    feed_mean,
    feed_square,
    down_weight,
    down_mean,
    down_square,
):
    n = ring_size
    block, depth = layer_input.shape
    length = n * block
    width = qkv_bias.shape[1]
    units = feed_weight.shape[2]
    place = lax.axis_index("tensor")
    ring = [(i, (i + 1) % n) for i in range(n)]

    def after(value, *others):
        return lax.optimization_barrier((value, *others))[0]

    def pass_on(values, pairs=ring):
        return lax.ppermute(values, "tensor", pairs)

    def pass_up(values, first, last):
        return pass_on(values, [(i, i + 1) for i in range(first, last + 1)])

    def pass_down(values, first, last):
        return pass_on(values, [(i, i - 1) for i in range(first, last + 1)])

    def at_place(table):
        return jnp.asarray(table, jnp.int32)[place]

    def plus(term, moving):
        return (term + moving.astype(F32)).astype(BF16)

    arrivals = [
        sorted(
            [(d, 0) for d in range(1, z + 1)] + [(d, 1) for d in range(1, n - z)]
        )
        for z in range(n)
    ]

    def where_of(blocks_of_place):
        mine = at_place(blocks_of_place)
        return jnp.stack([mine, lax.rem(place + n - mine, n), place]).astype(jnp.int32)

    def gather_weight(shard, axis):
        return lax.all_gather(shard.astype(BF16), "dp", axis=axis, tiled=True)

    def apart(*values):
        return lax.optimization_barrier(values)

    inputs = layer_input.astype(F32)
    w_qkv = gather_weight(qkv_weight.transpose(0, 2, 1), 2).reshape(3 * width, depth)
    w_proj = gather_weight(proj_weight, 1)
    w_feed = gather_weight(feed_weight, 1)
    w_down = gather_weight(down_weight, 1)
    normed_one, unit_one, inverse_one = norm_forward(inputs, norm_gain[0], norm_shift[0])
    starts = run_starts(segment_ids)
    cosine, sine = rotary_tables(starts)
    wheres = [where_of([(z - p) % n for z in range(n)]) for p in range(n)]

    wheres_back = [where_of(list(range(n)))] + [
        where_of([z + d if above else z - d for z, (d, above) in enumerate(column)])
        for column in zip(*arrivals)
    ]

    rows_one = [normed_one.astype(BF16)]
    buffer = None
    for p in range(n):
        if p < n - 1:
            moved = pass_on(rows_one[p])
            rows_one.append(
                after(moved, cosine, sine, starts, *wheres, *wheres_back) if p == 0 else moved
            )
        pre = contract(rows_one[p], w_qkv, 1, 1) + qkv_bias.reshape(1, 3 * width)
        buffer = rope_block(wheres[p], pre, cosine, sine, buffer, width, length)

    cotangent = after(output_grad, rows_one[n - 1])
    grad_up, grad_down_way = [cotangent], [cotangent]
    for hop in range(1, n):
        grad_up.append(pass_up(grad_up[hop - 1], hop - 1, n - 2))
        grad_down_way.append(pass_down(grad_down_way[hop - 1], 1, n - hop))

    mixed, totals, parts, lows = [None] * n, [None] * n, [None] * n, [None] * n
    gate = None
    for p in [1, *range(n - 1, 1, -1), 0]:
        where = wheres[p] if gate is None else after(wheres[p], gate)
        mixed[p], totals[p] = attend_block(where, starts, buffer, block)
        term = contract(mixed[p], w_proj, 0, 0)
        parts[p], lows[p] = apart(term, term.astype(BF16)) if p in (1, n - 1) else (term, None)
        gate = parts[p]

    def scatter_chains(parts, lows, gate=()):
        up = down = None
        for step in range(n - 1):
            term_up, term_down = parts[step + 1], parts[n - 1 - step]
            send_up = lows[1] if up is None else plus(term_up, up)
            send_down = lows[n - 1] if down is None else plus(term_down, after(down, send_up))
            if step == 0 and gate:
                send_up, send_down = after(send_up, *gate), after(send_down, *gate)
            up = pass_up(send_up, 0, step)
            down = pass_down(send_down, n - 1 - step, n - 1)
        return parts[0] + up.astype(F32) + down.astype(F32)

    middle = inputs + scatter_chains(parts, lows)
    grad_rows = [output_grad] + [
        jnp.where(place >= p, grad_up[p], grad_down_way[n - p]) for p in range(1, n)
    ]

    normed_two, unit_two, inverse_two = norm_forward(middle, norm_gain[1], norm_shift[1])
    rows_two = [normed_two.astype(BF16)]
    hidden, gate_grads, upper_grads, out_parts, back_parts = [], [], [], [], []
    out_lows, back_lows = [], []
    for p in range(n):
        if p < n - 1:
            rows_two.append(pass_on(rows_two[p]))
        gate = jnp.dot(rows_two[p], w_feed[0], preferred_element_type=F32)
        upper = jnp.dot(rows_two[p], w_feed[1], preferred_element_type=F32)
        grad_hidden = contract(grad_rows[p], w_down, 1, 1)
        sigma = jax.nn.sigmoid(gate)
        swish = gate * sigma
        hidden_low = (swish * upper).astype(BF16)
        gate_low = (grad_hidden * upper * sigma * (1.0 + gate * (1.0 - sigma))).astype(BF16)
        upper_low = (grad_hidden * swish).astype(BF16)
        hidden_low, gate_low, upper_low = apart(hidden_low, gate_low, upper_low)
        hidden.append(hidden_low)
        gate_grads.append(gate_low)
        upper_grads.append(upper_low)
        term = contract(gate_low, w_feed[0], 1, 1) + contract(upper_low, w_feed[1], 1, 1)
        if p == 1:
            term, low = apart(term, term.astype(BF16))
        else:
            (term,), low = apart(term), None
        back_parts.append(term)
        back_lows.append(low)
        term = jnp.dot(hidden_low, w_down, preferred_element_type=F32)
        if p in (1, n - 1):
            term, low = apart(term, term.astype(BF16))
        else:
            (term,), low = apart(term), None
        out_parts.append(term)
        out_lows.append(low)

    def scatter_sum(grad, axis):
        return lax.psum_scatter(grad, "dp", scatter_dimension=axis, tiled=True).astype(F32)

    grad_down = contract(
        jnp.concatenate(hidden, axis=0), jnp.concatenate(grad_rows, axis=0), 0, 0
    ).astype(BF16)
    down_sum = scatter_sum(grad_down, 1)
    grad_feed = jnp.einsum(
        "rd,krf->kdf",
        jnp.concatenate(rows_two, axis=0),
        jnp.concatenate(gate_grads + upper_grads, axis=0).reshape(2, length, units),
        preferred_element_type=F32,
    ).astype(BF16)
    feed_sum = scatter_sum(grad_feed, 1)

    moving = None
    for step in range(1, n):
        send = back_lows[step] if moving is None else plus(back_parts[step], moving)
        moving = pass_on(send)
    grad_normed_two = back_parts[0] + moving.astype(F32)

    grad_middle = output_grad.astype(F32) + norm_backward(
        grad_normed_two, unit_two, inverse_two, norm_gain[1]
    )
    gain_two = jnp.sum(grad_normed_two * unit_two, axis=0)
    shift_two = jnp.sum(grad_normed_two, axis=0)

    own = grad_middle.astype(BF16)
    ups, downs = [own], [own]
    all_totals = jnp.concatenate(totals, axis=0)
    slots, before = [own], None

    def back_block(slot, last):
        grad_mixed = contract(w_proj, slots[slot], 1, 1).astype(BF16)
        return attend_back_block(
            wheres_back[slot],
            starts,
            cosine,
            sine,
            buffer,
            grad_mixed,
            all_totals,
            before,
            last,
        )

    for hop in range(1, n):
        ups.append(pass_up(ups[hop - 1], hop - 1, n - 2))
        downs.append(pass_down(downs[hop - 1], 1, n - hop))
        before = back_block(hop - 1, False)
        chosen, here = None, after(place, slots[hop - 1])
        for z in range(n):
            d, above = arrivals[z][hop - 1]
            value = downs[d] if above else ups[d]
            chosen = value if chosen is None else jnp.where(here == z, value, chosen)
        slots.append(apart(chosen)[0])
    grad_pre = back_block(n - 1, True)
    layer_output = middle + scatter_chains(out_parts, out_lows, (ups[1], downs[1]))

    flat_pre = grad_pre.reshape(3 * width, length)
    moving = None
    for step in [*range(1, n), 0]:
        term = contract(flat_pre[:, step * block : (step + 1) * block], w_qkv, 0, 0)
        if step == 0:
            grad_normed_one = term + moving.astype(F32)
        else:
            send = term.astype(BF16) if moving is None else plus(term, moving)
            moving = pass_on(send)
    grad_qkv = contract(flat_pre, jnp.concatenate(rows_one, axis=0), 1, 0).astype(BF16)
    all_mixed = jnp.concatenate(mixed, axis=1)
    mixed_slots = []
    for slot in range(n):
        at = [0] * n if slot == 0 else [
            (-d if above else d) % n for d, above in (arrivals[z][slot - 1] for z in range(n))
        ]
        mixed_slots.append(
            lax.dynamic_slice_in_dim(all_mixed, at_place(at) * block, block, 1)
        )
    grad_proj = contract(
        jnp.concatenate(mixed_slots, axis=1), jnp.concatenate(slots, axis=0), 1, 0
    ).astype(BF16)
    grad_both = jnp.concatenate([grad_qkv, grad_proj], axis=0)
    both_rows = scatter_sum(grad_both, 1)
    qkv_sum = both_rows[: 3 * width].reshape(3, width, depth // data_size).transpose(0, 2, 1)
    proj_sum = both_rows[3 * width :]

    bias_local = jnp.sum(grad_pre.astype(F32), axis=2)
    input_grad = grad_middle + norm_backward(grad_normed_one, unit_one, inverse_one, norm_gain[0])
    gain_one = jnp.sum(grad_normed_one * unit_one, axis=0)
    shift_one = jnp.sum(grad_normed_one, axis=0)

    def sum_over(values, axis, size):
        step = 1
        while step < size:
            values = values + lax.ppermute(values, axis, [(i, i ^ step) for i in range(size)])
            step *= 2
        return values

    small = jnp.concatenate(
        [gain_one, gain_two, shift_one, shift_two, bias_local.reshape(3 * width)]
    )
    small = sum_over(small.reshape(-1, 128), "dp", data_size).reshape(-1)
    bias_grad = small[4 * depth :].reshape(3, width)
    small = sum_over(small[: 4 * depth].reshape(-1, 128), "tensor", n)
    gain_total, shift_total = small.reshape(2, 2, depth)

    outputs = [layer_output, input_grad]
    groups = (
        (norm_gain, gain_total, gain_mean, gain_square),
        (norm_shift, shift_total, shift_mean, shift_square),
        (qkv_bias, bias_grad, bias_mean, bias_square),
        (qkv_weight, qkv_sum, qkv_mean, qkv_square),
        (proj_weight, proj_sum, proj_mean, proj_square),
        (feed_weight, feed_sum, feed_mean, feed_square),
        (down_weight, down_sum, down_mean, down_square),
    )
    for which, (param_arr, grad_total, mean_in, square_in) in enumerate(groups):
        change, mean_new, square_new = adamw(param_arr, grad_total, mean_in, square_in)
        shown = change if which < 3 else param_arr + change
        outputs.extend([grad_total, shown, mean_new, square_new])
    return tuple(outputs)


def solution(mesh):
    tokens, small, bias = P(("dp", "tensor"), None), P(), P(None, "tensor")
    three, two = P(None, "dp", "tensor"), P("tensor", "dp")
    per_param = [small] * 6 + [bias] * 3 + [three] * 3 + [two] * 3 + [three] * 3 + [two] * 3
    outs = [small] * 8 + [bias] * 4 + [three] * 4 + [two] * 4 + [three] * 4 + [two] * 4
    n = mesh.shape["tensor"]

    def body(*args):
        return per_device(n, mesh.shape["dp"], *args)

    return jax.shard_map(
        body,
        mesh=mesh,
        in_specs=(tokens, tokens, P("dp", None), *per_param),
        out_specs=(tokens, tokens, *outs),
        check_vma=False,
    )
```

```python
import functools
import math

import jax
import jax.numpy as jnp
from jax import lax
from jax.experimental import pallas as pl
from jax.experimental.layout import Layout, with_layout_constraint
from jax.experimental.pallas import tpu as pltpu
from jax.sharding import PartitionSpec as P


HEAD = 64
ROT = 16
HALF = ROT // 2
STEP = 10
PAIR = 2
WIDE = 4
MASKED = -1000000000.0
BF16 = jnp.bfloat16
F32 = jnp.float32

norm_eps = 1e-05


def norm_forward(values, gain_row, shift_row):
    center = values - jnp.mean(values, axis=-1, keepdims=True)
    inverse = lax.rsqrt(jnp.mean(center * center, axis=-1, keepdims=True) + norm_eps)
    unit_rows = center * inverse
    return (unit_rows * gain_row + shift_row, unit_rows, inverse)


def norm_backward(grad_in, unit_rows, inverse, gain_row):
    scaled = grad_in * gain_row
    return inverse * (
        scaled
        - jnp.mean(scaled, axis=-1, keepdims=True)
        - unit_rows * jnp.mean(scaled * unit_rows, axis=-1, keepdims=True)
    )


def run_starts(segments):
    token_index = jnp.arange(segments.shape[1], dtype=jnp.int32)[None, :]
    starts = jnp.concatenate(
        [jnp.ones((1, 1), dtype=bool), segments[:, 1:] != segments[:, :-1]], axis=1
    )
    return lax.cummax(jnp.where(starts, token_index, 0), axis=1)


def rotary_tables(starts):
    token_index = jnp.arange(starts.shape[1], dtype=jnp.int32)[None, :]
    freqs = jnp.exp(jnp.arange(HALF, dtype=F32) * (-2.0 * math.log(10000.0) / ROT))
    angles = (token_index - starts).astype(F32) * freqs[:, None]
    return (jnp.cos(angles), jnp.sin(angles))


def adamw(param, grad_in, mean_in, square_in):
    mean_new = 0.9 * mean_in + 0.1 * grad_in
    square_new = 0.95 * square_in + 0.05 * grad_in * grad_in
    corrected = mean_new / (1.0 - 0.9**STEP)
    scaled = jnp.sqrt(square_new / (1.0 - 0.95**STEP)) + 1e-08
    change = -0.02 * (corrected / scaled + 0.1 * param)
    return (change, mean_new, square_new)


def contract(left, right, left_dim, right_dim):
    return lax.dot_general(
        left, right, (((left_dim,), (right_dim,)), ((), ())), preferred_element_type=F32
    )


def rope_kernel(where_ref, q_ref, k_ref, v_ref, cos_ref, sin_ref, old_ref, out_ref):
    del where_ref, old_ref
    cosine, sine = cos_ref[...], sin_ref[...]
    for which, ref in enumerate((q_ref, k_ref, v_ref)):
        whole = ref[...].T
        for head in range(WIDE):
            rows = slice(head * HEAD, (head + 1) * HEAD)
            part = whole[rows]
            if which < 2:
                first, second = part[:HALF], part[HALF:ROT]
                part = jnp.concatenate(
                    [
                        first * cosine - second * sine,
                        second * cosine + first * sine,
                        part[ROT:],
                    ],
                    axis=0,
                )
            if which == 0:
                part = part * (HEAD**-0.5)
            out_ref[which, rows, :] = part.astype(BF16)


def rope_block(where, base, pre, cosine, sine, buffer, width, length):
    rows = WIDE * HEAD
    groups = width // rows
    block = pre.shape[0]
    first = buffer is None
    body = rope_kernel
    specs = [
        pl.BlockSpec((block, rows), lambda h, s: (0, h)),
        pl.BlockSpec((block, rows), lambda h, s: (0, groups + h)),
        pl.BlockSpec((block, rows), lambda h, s: (0, 2 * groups + h)),
        pl.BlockSpec((HALF, block), lambda h, s: (0, s[base])),
        pl.BlockSpec((HALF, block), lambda h, s: (0, s[base])),
    ]
    args = [where, pre, pre, pre, cosine, sine]
    aliases = {}
    if first:
        body = lambda w, q, k, v, c, d, o: rope_kernel(w, q, k, v, c, d, None, o)
    else:
        specs.append(pl.BlockSpec(memory_space=pl.ANY))
        aliases = {len(args): 0}
        args.append(buffer)
    return pl.pallas_call(
        body,
        out_shape=jax.ShapeDtypeStruct((3, width, length), BF16),
        grid_spec=pltpu.PrefetchScalarGridSpec(
            num_scalar_prefetch=1,
            grid=(groups,),
            in_specs=specs,
            out_specs=pl.BlockSpec((3, rows, block), lambda h, s: (0, h, s[base])),
        ),
        input_output_aliases=aliases,
        cost_estimate=pl.CostEstimate(
            flops=6 * 3 * width * block, bytes_accessed=18 * width * block, transcendentals=0
        ),
        name="rope_block",
    )(*args)


def allowed(key_block, query_block, block, starts):
    shape = (block, block)
    key_at = lax.broadcasted_iota(jnp.int32, shape, 0) + key_block * block
    mask = key_at >= starts
    if key_block == query_block:
        query_at = lax.broadcasted_iota(jnp.int32, shape, 1) + query_block * block
        mask = mask & (key_at <= query_at)
    return mask


def attend_kernel(blocks, block, base, where_ref, starts_ref, q_ref, k_ref, v_ref, out_ref, total_ref):
    starts = starts_ref[...]
    for mine in range(blocks):

        @pl.when(where_ref[base] == mine)
        def _(mine=mine):
            for head in range(PAIR):
                rows = slice(head * HEAD, (head + 1) * HEAD)
                query = q_ref[0, rows, :]
                scores = []
                for other in range(mine + 1):
                    keys = k_ref[0, rows, other * block : (other + 1) * block]
                    raw = contract(keys, query, 0, 0)
                    scores.append(jnp.where(allowed(other, mine, block, starts), raw, MASKED))
                top = functools.reduce(
                    jnp.maximum, [jnp.max(s, axis=0, keepdims=True) for s in scores]
                )
                total = jnp.zeros((1, block), F32)
                result = jnp.zeros((HEAD, block), F32)
                for other, s in enumerate(scores):
                    terms = jnp.exp(s - top)
                    total = total + jnp.sum(terms, axis=0, keepdims=True)
                    values = v_ref[0, rows, other * block : (other + 1) * block]
                    result = result + contract(values, terms.astype(BF16), 1, 0)
                out_ref[rows, :] = (result / total).astype(BF16)
                total_ref[head] = top + jnp.log(total)


def attend_block(where, base, starts, buffer, block):
    _, width, length = buffer.shape
    rows = PAIR * HEAD
    heads, blocks = width // HEAD, length // block
    return pl.pallas_call(
        functools.partial(attend_kernel, blocks, block, base),
        out_shape=(
            jax.ShapeDtypeStruct((width, block), BF16),
            jax.ShapeDtypeStruct((heads, 1, block), F32),
        ),
        grid_spec=pltpu.PrefetchScalarGridSpec(
            num_scalar_prefetch=1,
            grid=(width // rows,),
            in_specs=[
                pl.BlockSpec((1, block), lambda h, s: (0, s[base])),
                pl.BlockSpec((1, rows, block), lambda h, s: (0, h, s[base])),
                pl.BlockSpec((1, rows, length), lambda h, s: (1, h, 0)),
                pl.BlockSpec((1, rows, length), lambda h, s: (2, h, 0)),
            ],
            out_specs=(
                pl.BlockSpec((rows, block), lambda h, s: (h, 0)),
                pl.BlockSpec((PAIR, 1, block), lambda h, s: (h, 0, 0)),
            ),
        ),
        cost_estimate=pl.CostEstimate(
            flops=16 * width * block * length,
            bytes_accessed=2 * width * (2 * length + 2 * block),
            transcendentals=heads * block * length,
        ),
        name="attend_block",
    )(where, starts, buffer, buffer, buffer)


def attend_back_kernel(blocks, block, base, first, last, where_ref, starts_ref, cos_ref, sin_ref, *refs):
    if last:
        all_cos_ref, all_sin_ref, *refs = refs
    q_ref, k_ref, v_ref, grad_ref, total_ref, *refs = refs
    if not first:
        old_out_ref, old_ref, *refs = refs
    if last:
        (out_ref,) = refs
    else:
        out_ref, sums_ref = refs
    starts = starts_ref[...]
    cosine, sine = cos_ref[...], sin_ref[...]

    def unrotate(part, cosine, sine):
        one, two = part[:HALF], part[HALF:ROT]
        return jnp.concatenate(
            [one * cosine + two * sine, two * cosine - one * sine, part[ROT:]], axis=0
        )

    def at_position(position):
        return pl.ds(pl.multiple_of(position * block, block), block)

    if last:
        for position in range(blocks):
            columns = slice(position * block, (position + 1) * block)
            out_ref[0, :, columns] = old_out_ref[:, columns]

    for mine in range(blocks):

        @pl.when(where_ref[base] == mine)
        def _(mine=mine):
            for head in range(PAIR):
                rows = slice(head * HEAD, (head + 1) * HEAD)
                query = q_ref[0, rows, :]
                grad = grad_ref[rows, :]
                row_total = total_ref[head]
                kept = []
                offset = jnp.zeros((1, block), F32)
                for other in range(mine + 1):
                    columns = slice(other * block, (other + 1) * block)
                    raw = contract(k_ref[0, rows, columns], query, 0, 0)
                    masked = jnp.where(allowed(other, mine, block, starts), raw, MASKED)
                    weights = jnp.exp(masked - row_total)
                    back = contract(v_ref[0, rows, columns], grad, 0, 0)
                    offset = offset + jnp.sum(weights * back, axis=0, keepdims=True)
                    kept.append((weights, back))
                query_sum = jnp.zeros((HEAD, block), F32)
                for other in range(blocks):
                    columns = slice(other * block, (other + 1) * block)
                    if other <= mine:
                        weights, back = kept[other]
                        change = (weights * (back - offset)).astype(BF16)
                        query_sum = query_sum + contract(k_ref[0, rows, columns], change, 1, 0)
                        key_sum = contract(query, change, 1, 1)
                        value_sum = contract(grad, weights.astype(BF16), 1, 1)
                        if not first:
                            key_sum = key_sum + old_ref[0, rows, columns]
                            value_sum = value_sum + old_ref[1, rows, columns]
                    elif first:
                        key_sum = jnp.zeros((HEAD, block), F32)
                        value_sum = jnp.zeros((HEAD, block), F32)
                    else:
                        key_sum = old_ref[0, rows, columns]
                        value_sum = old_ref[1, rows, columns]
                    if last:
                        there = at_position(lax.rem(where_ref[base + 2] + blocks - other, blocks))
                        turned = unrotate(
                            key_sum, all_cos_ref[:, columns], all_sin_ref[:, columns]
                        )
                        out_ref[1, rows, there] = turned.astype(BF16)
                        out_ref[2, rows, there] = value_sum.astype(BF16)
                    else:
                        sums_ref[0, rows, columns] = key_sum
                        sums_ref[1, rows, columns] = value_sum
                query_sum = unrotate(query_sum * (HEAD**-0.5), cosine, sine).astype(BF16)
                if last:
                    out_ref[0, rows, at_position(where_ref[base + 1])] = query_sum
                else:
                    out_ref[rows, :] = query_sum


def attend_back_block(where, base, starts, cosine, sine, buffer, grad, totals, before, last):
    _, width, length = buffer.shape
    block = grad.shape[1]
    rows = PAIR * HEAD
    heads, blocks = width // HEAD, length // block
    groups = width // rows
    first = before is None
    whole_table = pl.BlockSpec((HALF, length), lambda h, s: (0, 0))
    both = pl.BlockSpec((2, rows, length), lambda h, s: (0, h, 0))
    specs = [
        pl.BlockSpec((1, block), lambda h, s: (0, s[base])),
        pl.BlockSpec((HALF, block), lambda h, s: (0, s[base])),
        pl.BlockSpec((HALF, block), lambda h, s: (0, s[base])),
    ]
    args = [where, starts, cosine, sine]
    if last:
        specs += [whole_table, whole_table]
        args += [cosine, sine]
    specs += [
        pl.BlockSpec((1, rows, block), lambda h, s: (0, h, s[base])),
        pl.BlockSpec((1, rows, length), lambda h, s: (1, h, 0)),
        pl.BlockSpec((1, rows, length), lambda h, s: (2, h, 0)),
        pl.BlockSpec((rows, block), lambda h, s: (h, 0)),
        pl.BlockSpec((PAIR, 1, block), lambda h, s: (s[base + 3] * groups + h, 0, 0)),
    ]
    args += [buffer, buffer, buffer, grad, totals]
    aliases = {}
    if not first:
        if last:
            specs += [pl.BlockSpec((rows, length), lambda h, s: (h, 0)), both]
        else:
            specs += [pl.BlockSpec(memory_space=pl.ANY), both]
            aliases = {len(args): 0, len(args) + 1: 1}
        args += before
    if last:
        out_shape = jax.ShapeDtypeStruct((3, width, length), BF16)
        out_specs = pl.BlockSpec((3, rows, length), lambda h, s: (0, h, 0))
    else:
        out_shape = (
            jax.ShapeDtypeStruct((width, length), BF16),
            jax.ShapeDtypeStruct((2, width, length), F32),
        )
        out_specs = (pl.BlockSpec((rows, block), lambda h, s: (h, s[base + 1])), both)
    return pl.pallas_call(
        functools.partial(attend_back_kernel, blocks, block, base, first, last),
        out_shape=out_shape,
        grid_spec=pltpu.PrefetchScalarGridSpec(
            num_scalar_prefetch=1, grid=(groups,), in_specs=specs, out_specs=out_specs
        ),
        input_output_aliases=aliases,
        cost_estimate=pl.CostEstimate(
            flops=40 * width * block * length,
            bytes_accessed=2 * width * (10 * length + 3 * block),
            transcendentals=heads * block * length,
        ),
        name="attend_back_block",
    )(*args)


def per_device(
    ring_size,
    data_size,
    layer_input,
    output_grad,
    segment_ids,
    norm_gain,
    gain_mean,
    gain_square,
    norm_shift,
    shift_mean,
    shift_square,
    qkv_bias,
    bias_mean,
    bias_square,
    qkv_weight,
    qkv_mean,
    qkv_square,
    proj_weight,
    proj_mean,
    proj_square,
    feed_weight,
    feed_mean,
    feed_square,
    down_weight,
    down_mean,
    down_square,
):
    n = ring_size
    block, depth = layer_input.shape
    length = n * block
    width = qkv_bias.shape[1]
    units = feed_weight.shape[2]
    place = lax.axis_index("tensor")
    ring = [(i, (i + 1) % n) for i in range(n)]

    def after(value, *others):
        return lax.optimization_barrier((value, *others))[0]

    def pass_on(values, pairs=ring):
        return lax.ppermute(values, "tensor", pairs)

    def pass_up(values, first, last):
        return pass_on(values, [(i, i + 1) for i in range(first, last + 1)])

    def pass_down(values, first, last):
        return pass_on(values, [(i, i - 1) for i in range(first, last + 1)])

    def plus(term, moving):
        return (term + moving.astype(F32)).astype(BF16)

    arrivals = [
        sorted(
            [(d, 0) for d in range(1, z + 1)] + [(d, 1) for d in range(1, n - z)]
        )
        for z in range(n)
    ]

    taken = [
        sorted(range(1, n), key=lambda p: (p - 1 if p > z else n - 1 - p, p)) + [0]
        for z in range(n)
    ]

    def where_row(z):
        blocks = [(z - p) % n for p in range(n)] + [(z - p) % n for p in taken[z]]
        blocks += [z] + [z + d if above else z - d for d, above in arrivals[z]]
        return [
            v for b in blocks for v in (b, (z - b) % n, z, taken[z].index((z - b) % n))
        ]

    where = jnp.asarray([where_row(z) for z in range(n)], jnp.int32)[place]

    def choose(values, ranks):
        groups = sorted(set(ranks.values()))
        result = values[groups[0]]
        for rank in groups[1:]:
            here = functools.reduce(
                jnp.logical_or, [place == z for z, r in ranks.items() if r == rank]
            )
            result = jnp.where(here, values[rank], result)
        return result

    def gather_weight(shard, axis):
        return lax.all_gather(shard.astype(BF16), "dp", axis=axis, tiled=True)

    def apart(*values):
        return lax.optimization_barrier(values)

    inputs = layer_input.astype(F32)
    w_qkv = gather_weight(qkv_weight.transpose(0, 2, 1), 2).reshape(3 * width, depth)
    w_proj = gather_weight(proj_weight, 1)
    w_feed = gather_weight(feed_weight, 1)
    w_down = gather_weight(down_weight, 1)
    normed_one, unit_one, inverse_one = norm_forward(inputs, norm_gain[0], norm_shift[0])
    starts = run_starts(segment_ids)
    cosine, sine = rotary_tables(starts)
    rows_one = [normed_one.astype(BF16)]
    buffer = None
    for p in range(n):
        if p < n - 1:
            moved = pass_on(rows_one[p])
            rows_one.append(
                after(moved, cosine, sine, starts, where)
                if p == 0
                else moved
            )
        pre = contract(rows_one[p], w_qkv, 1, 1) + qkv_bias.reshape(1, 3 * width)
        buffer = rope_block(where, 4 * p, pre, cosine, sine, buffer, width, length)

    cotangent = after(output_grad, rows_one[n - 1])
    grad_up, grad_down_way = [cotangent], [cotangent]
    for hop in range(1, n):
        grad_up.append(pass_up(grad_up[hop - 1], hop - 1, n - 2))
        grad_down_way.append(pass_down(grad_down_way[hop - 1], 1, n - hop))

    mixed, totals, parts = [], [], []
    for rank in range(n):
        at = after(where, parts[-1]) if rank else where
        mixed_one, totals_one = attend_block(at, 4 * (n + rank), starts, buffer, block)
        mixed.append(mixed_one)
        totals.append(totals_one)
        term = contract(mixed_one, w_proj, 0, 0)
        parts.append(apart(term.astype(BF16) if rank < n - 1 else term)[0])

    def scatter_chains(parts, rank_of, gate=()):
        first = choose(parts, {0: rank_of(0, 1), n - 1: rank_of(n - 1, n - 1)})
        up = down = pass_on(after(first, *gate), [(0, 1), (n - 1, n - 2)])
        for step in range(1, n - 1):
            up_ranks = {z: rank_of(z, step + 1) for z in range(step + 1)}
            down_ranks = {z: rank_of(z, n - 1 - step) for z in range(n - 1 - step, n)}
            send_up = plus(choose(parts, up_ranks).astype(F32), up)
            send_down = plus(
                choose(parts, down_ranks).astype(F32), after(down, send_up)
            )
            up = pass_up(send_up, 0, step)
            down = pass_down(send_down, n - 1 - step, n - 1)
        return parts[rank_of(0, 0)].astype(F32) + up.astype(F32) + down.astype(F32)

    middle = inputs + scatter_chains(parts, lambda z, p: taken[z].index(p))
    grad_rows = [output_grad] + [
        jnp.where(place >= p, grad_up[p], grad_down_way[n - p]) for p in range(1, n)
    ]

    normed_two, unit_two, inverse_two = norm_forward(middle, norm_gain[1], norm_shift[1])
    rows_two = [normed_two.astype(BF16)]
    for hop in range(1, n):
        rows_two.append(pass_on(rows_two[hop - 1]))
    halves = [range(n // 2), range(n // 2, n)]
    rows_half, grad_half, hidden, gate_grads, upper_grads = [], [], [], [], []
    out_parts, back_parts = [], []
    for half in halves:
        rows_here, grads_here = apart(
            jnp.concatenate([rows_two[p] for p in half], axis=0),
            jnp.concatenate([grad_rows[p] for p in half], axis=0),
        )
        rows_half.append(rows_here)
        grad_half.append(grads_here)
        gate = jnp.dot(rows_here, w_feed[0], preferred_element_type=F32)
        upper = jnp.dot(rows_here, w_feed[1], preferred_element_type=F32)
        grad_hidden = contract(grads_here, w_down, 1, 1)
        sigma = jax.nn.sigmoid(gate)
        swish = gate * sigma
        hidden_low = (swish * upper).astype(BF16)
        gate_low = (grad_hidden * upper * sigma * (1.0 + gate * (1.0 - sigma))).astype(BF16)
        upper_low = (grad_hidden * swish).astype(BF16)
        hidden_low, gate_low, upper_low = apart(hidden_low, gate_low, upper_low)
        hidden.append(hidden_low)
        gate_grads.append(gate_low)
        upper_grads.append(upper_low)
        term = contract(gate_low, w_feed[0], 1, 1) + contract(upper_low, w_feed[1], 1, 1)
        (term,) = apart(term)
        back_parts.extend(jnp.split(term, len(half), axis=0))
        (term,) = apart(jnp.dot(hidden_low, w_down, preferred_element_type=F32).astype(BF16))
        out_parts.extend(jnp.split(term, len(half), axis=0))

    def scatter_sum(grad, axis):
        return lax.psum_scatter(grad, "dp", scatter_dimension=axis, tiled=True)

    grad_down = contract(
        jnp.concatenate(hidden, axis=0), jnp.concatenate(grad_half, axis=0), 0, 0
    ).astype(BF16)
    down_sum = scatter_sum(grad_down, 1).astype(F32)
    grad_feed = jnp.einsum(
        "krf,rd->kfd",
        jnp.concatenate(gate_grads + upper_grads, axis=0).reshape(2, length, units),
        jnp.concatenate(rows_half, axis=0),
        preferred_element_type=F32,
    ).astype(BF16)
    feed_sum = with_layout_constraint(
        scatter_sum(grad_feed, 2).transpose(0, 2, 1), Layout((0, 1, 2))
    ).astype(F32)

    moving = None
    for step in range(1, n):
        if moving is None:
            send = after(back_parts[step].astype(BF16), rows_two[n - 1])
        else:
            send = plus(back_parts[step], moving)
        moving = pass_on(send)
    grad_normed_two = back_parts[0] + moving.astype(F32)

    grad_middle = output_grad.astype(F32) + norm_backward(
        grad_normed_two, unit_two, inverse_two, norm_gain[1]
    )
    gain_two = jnp.sum(grad_normed_two * unit_two, axis=0)
    shift_two = jnp.sum(grad_normed_two, axis=0)

    own = grad_middle.astype(BF16)
    ups, downs = [own], [own]
    all_totals = jnp.concatenate(totals, axis=0)
    slots, before = [own], None

    def back_block(slot, last):
        grad_mixed = contract(w_proj, slots[slot], 1, 1).astype(BF16)
        return attend_back_block(
            where,
            4 * (2 * n + slot),
            starts,
            cosine,
            sine,
            buffer,
            grad_mixed,
            all_totals,
            before,
            last,
        )

    for hop in range(1, n):
        ups.append(pass_up(ups[hop - 1], hop - 1, n - 2))
        downs.append(pass_down(downs[hop - 1], 1, n - hop))
        before = back_block(hop - 1, False)
        chosen, here = None, after(place, slots[hop - 1])
        for z in range(n):
            d, above = arrivals[z][hop - 1]
            value = downs[d] if above else ups[d]
            chosen = value if chosen is None else jnp.where(here == z, value, chosen)
        slots.append(apart(chosen)[0])
    grad_pre = back_block(n - 1, True)
    layer_output = middle + scatter_chains(out_parts, lambda z, p: p, (ups[1], downs[1]))

    flat_pre = grad_pre.reshape(3 * width, length)
    moving, first_parts = None, [None] * n
    for step in [*range(1, n), 0]:
        term = contract(flat_pre[:, step * block : (step + 1) * block], w_qkv, 0, 0)
        first_parts[step] = apart(term.astype(BF16) if step == 1 else term)[0]
    for step in range(1, n):
        send = first_parts[1] if moving is None else plus(first_parts[step], moving)
        moving = pass_on(send)
    grad_normed_one = first_parts[0] + moving.astype(F32)
    grad_qkv = contract(flat_pre, jnp.concatenate(rows_one, axis=0), 1, 0).astype(BF16)
    all_mixed = jnp.concatenate(mixed, axis=1)
    mixed_slots = [
        lax.dynamic_slice_in_dim(all_mixed, where[4 * (2 * n + slot) + 3] * block, block, 1)
        for slot in range(n)
    ]
    grad_proj = contract(
        jnp.concatenate(mixed_slots, axis=1), jnp.concatenate(slots, axis=0), 1, 0
    ).astype(BF16)
    grad_both = jnp.concatenate([grad_qkv, grad_proj], axis=0)
    both_rows = scatter_sum(grad_both, 1).astype(F32)
    qkv_sum = both_rows[: 3 * width].reshape(3, width, depth // data_size).transpose(0, 2, 1)
    proj_sum = both_rows[3 * width :]

    bias_local = jnp.sum(grad_pre.astype(F32), axis=2)
    input_grad = grad_middle + norm_backward(grad_normed_one, unit_one, inverse_one, norm_gain[0])
    gain_one = jnp.sum(grad_normed_one * unit_one, axis=0)
    shift_one = jnp.sum(grad_normed_one, axis=0)

    def sum_over(values, axis, size):
        step = 1
        while step < size:
            values = values + lax.ppermute(values, axis, [(i, i ^ step) for i in range(size)])
            step *= 2
        return values

    small = jnp.concatenate(
        [gain_one, gain_two, shift_one, shift_two, bias_local.reshape(3 * width)]
    )
    small = sum_over(small.reshape(-1, 128), "dp", data_size).reshape(-1)
    bias_grad = small[4 * depth :].reshape(3, width)
    small = sum_over(small[: 4 * depth].reshape(-1, 128), "tensor", n)
    gain_total, shift_total = small.reshape(2, 2, depth)

    outputs = [layer_output, input_grad]
    groups = (
        (norm_gain, gain_total, gain_mean, gain_square),
        (norm_shift, shift_total, shift_mean, shift_square),
        (qkv_bias, bias_grad, bias_mean, bias_square),
        (qkv_weight, qkv_sum, qkv_mean, qkv_square),
        (proj_weight, proj_sum, proj_mean, proj_square),
        (feed_weight, feed_sum, feed_mean, feed_square),
        (down_weight, down_sum, down_mean, down_square),
    )
    for which, (param_arr, grad_total, mean_in, square_in) in enumerate(groups):
        change, mean_new, square_new = adamw(param_arr, grad_total, mean_in, square_in)
        shown = change if which < 3 else param_arr + change
        outputs.extend([grad_total, shown, mean_new, square_new])
    return tuple(outputs)


def solution(mesh):
    tokens, small, bias = P(("dp", "tensor"), None), P(), P(None, "tensor")
    three, two = P(None, "dp", "tensor"), P("tensor", "dp")
    per_param = [small] * 6 + [bias] * 3 + [three] * 3 + [two] * 3 + [three] * 3 + [two] * 3
    outs = [small] * 8 + [bias] * 4 + [three] * 4 + [two] * 4 + [three] * 4 + [two] * 4
    n = mesh.shape["tensor"]

    def body(*args):
        return per_device(n, mesh.shape["dp"], *args)

    return jax.shard_map(
        body,
        mesh=mesh,
        in_specs=(tokens, tokens, P("dp", None), *per_param),
        out_specs=(tokens, tokens, *outs),
        check_vma=False,
    )
```

```python
import functools
import math

import jax
import jax.numpy as jnp
from jax import lax
from jax.experimental import pallas as pl
from jax.experimental.layout import Layout, with_layout_constraint
from jax.experimental.pallas import tpu as pltpu
from jax.sharding import PartitionSpec as P


HEAD = 64
ROT = 16
HALF = ROT // 2
STEP = 10
PAIR = 2
WIDE = 4
MASKED = -1000000000.0
BF16 = jnp.bfloat16
F32 = jnp.float32

norm_eps = 1e-05


def norm_forward(values, gain_row, shift_row):
    center = values - jnp.mean(values, axis=-1, keepdims=True)
    inverse = lax.rsqrt(jnp.mean(center * center, axis=-1, keepdims=True) + norm_eps)
    unit_rows = center * inverse
    return (unit_rows * gain_row + shift_row, unit_rows, inverse)


def norm_backward(grad_in, unit_rows, inverse, gain_row):
    scaled = grad_in * gain_row
    return inverse * (
        scaled
        - jnp.mean(scaled, axis=-1, keepdims=True)
        - unit_rows * jnp.mean(scaled * unit_rows, axis=-1, keepdims=True)
    )


def run_starts(segments):
    token_index = jnp.arange(segments.shape[1], dtype=jnp.int32)[None, :]
    starts = jnp.concatenate(
        [jnp.ones((1, 1), dtype=bool), segments[:, 1:] != segments[:, :-1]], axis=1
    )
    return lax.cummax(jnp.where(starts, token_index, 0), axis=1)


def rotary_tables(starts):
    token_index = jnp.arange(starts.shape[1], dtype=jnp.int32)[None, :]
    freqs = jnp.exp(jnp.arange(HALF, dtype=F32) * (-2.0 * math.log(10000.0) / ROT))
    angles = (token_index - starts).astype(F32) * freqs[:, None]
    return (jnp.cos(angles), jnp.sin(angles))


def adamw(param, grad_in, mean_in, square_in):
    mean_new = 0.9 * mean_in + 0.1 * grad_in
    square_new = 0.95 * square_in + 0.05 * grad_in * grad_in
    corrected = mean_new / (1.0 - 0.9**STEP)
    scaled = jnp.sqrt(square_new / (1.0 - 0.95**STEP)) + 1e-08
    change = -0.02 * (corrected / scaled + 0.1 * param)
    return (change, mean_new, square_new)


def contract(left, right, left_dim, right_dim):
    return lax.dot_general(
        left, right, (((left_dim,), (right_dim,)), ((), ())), preferred_element_type=F32
    )


def rope_kernel(where_ref, q_ref, k_ref, v_ref, cos_ref, sin_ref, old_ref, out_ref):
    del where_ref, old_ref
    cosine, sine = cos_ref[...], sin_ref[...]
    for which, ref in enumerate((q_ref, k_ref, v_ref)):
        whole = ref[...].T
        for head in range(WIDE):
            rows = slice(head * HEAD, (head + 1) * HEAD)
            part = whole[rows]
            if which < 2:
                first, second = part[:HALF], part[HALF:ROT]
                part = jnp.concatenate(
                    [
                        first * cosine - second * sine,
                        second * cosine + first * sine,
                        part[ROT:],
                    ],
                    axis=0,
                )
            if which == 0:
                part = part * (HEAD**-0.5)
            out_ref[which, rows, :] = part.astype(BF16)


def rope_block(where, base, pre, cosine, sine, buffer, width, length):
    rows = WIDE * HEAD
    groups = width // rows
    block = pre.shape[0]
    first = buffer is None
    body = rope_kernel
    specs = [
        pl.BlockSpec((block, rows), lambda h, s: (0, h)),
        pl.BlockSpec((block, rows), lambda h, s: (0, groups + h)),
        pl.BlockSpec((block, rows), lambda h, s: (0, 2 * groups + h)),
        pl.BlockSpec((HALF, block), lambda h, s: (0, s[base])),
        pl.BlockSpec((HALF, block), lambda h, s: (0, s[base])),
    ]
    args = [where, pre, pre, pre, cosine, sine]
    aliases = {}
    if first:
        body = lambda w, q, k, v, c, d, o: rope_kernel(w, q, k, v, c, d, None, o)
    else:
        specs.append(pl.BlockSpec(memory_space=pl.ANY))
        aliases = {len(args): 0}
        args.append(buffer)
    return pl.pallas_call(
        body,
        out_shape=jax.ShapeDtypeStruct((3, width, length), BF16),
        grid_spec=pltpu.PrefetchScalarGridSpec(
            num_scalar_prefetch=1,
            grid=(groups,),
            in_specs=specs,
            out_specs=pl.BlockSpec((3, rows, block), lambda h, s: (0, h, s[base])),
        ),
        input_output_aliases=aliases,
        cost_estimate=pl.CostEstimate(
            flops=6 * 3 * width * block, bytes_accessed=18 * width * block, transcendentals=0
        ),
        name="rope_block",
    )(*args)


def allowed(key_block, query_block, block, starts):
    shape = (block, block)
    key_at = lax.broadcasted_iota(jnp.int32, shape, 0) + key_block * block
    mask = key_at >= starts
    if key_block == query_block:
        query_at = lax.broadcasted_iota(jnp.int32, shape, 1) + query_block * block
        mask = mask & (key_at <= query_at)
    return mask


def attend_kernel(blocks, block, base, where_ref, starts_ref, q_ref, k_ref, v_ref, out_ref, total_ref):
    starts = starts_ref[...]
    for mine in range(blocks):

        @pl.when(where_ref[base] == mine)
        def _(mine=mine):
            for head in range(PAIR):
                rows = slice(head * HEAD, (head + 1) * HEAD)
                query = q_ref[0, rows, :]
                scores = []
                for other in range(mine + 1):
                    keys = k_ref[0, rows, other * block : (other + 1) * block]
                    raw = contract(keys, query, 0, 0)
                    scores.append(jnp.where(allowed(other, mine, block, starts), raw, MASKED))
                top = functools.reduce(
                    jnp.maximum, [jnp.max(s, axis=0, keepdims=True) for s in scores]
                )
                total = jnp.zeros((1, block), F32)
                result = jnp.zeros((HEAD, block), F32)
                for other, s in enumerate(scores):
                    terms = jnp.exp(s - top)
                    total = total + jnp.sum(terms, axis=0, keepdims=True)
                    values = v_ref[0, rows, other * block : (other + 1) * block]
                    result = result + contract(values, terms.astype(BF16), 1, 0)
                out_ref[rows, :] = (result / total).astype(BF16)
                total_ref[head] = top + jnp.log(total)


def attend_block(where, base, starts, buffer, block):
    _, width, length = buffer.shape
    rows = PAIR * HEAD
    heads, blocks = width // HEAD, length // block
    return pl.pallas_call(
        functools.partial(attend_kernel, blocks, block, base),
        out_shape=(
            jax.ShapeDtypeStruct((width, block), BF16),
            jax.ShapeDtypeStruct((heads, 1, block), F32),
        ),
        grid_spec=pltpu.PrefetchScalarGridSpec(
            num_scalar_prefetch=1,
            grid=(width // rows,),
            in_specs=[
                pl.BlockSpec((1, block), lambda h, s: (0, s[base])),
                pl.BlockSpec((1, rows, block), lambda h, s: (0, h, s[base])),
                pl.BlockSpec((1, rows, length), lambda h, s: (1, h, 0)),
                pl.BlockSpec((1, rows, length), lambda h, s: (2, h, 0)),
            ],
            out_specs=(
                pl.BlockSpec((rows, block), lambda h, s: (h, 0)),
                pl.BlockSpec((PAIR, 1, block), lambda h, s: (h, 0, 0)),
            ),
        ),
        cost_estimate=pl.CostEstimate(
            flops=16 * width * block * length,
            bytes_accessed=2 * width * (2 * length + 2 * block),
            transcendentals=heads * block * length,
        ),
        name="attend_block",
    )(where, starts, buffer, buffer, buffer)


def attend_back_kernel(blocks, block, base, first, last, where_ref, starts_ref, cos_ref, sin_ref, *refs):
    if last:
        all_cos_ref, all_sin_ref, *refs = refs
    q_ref, k_ref, v_ref, grad_ref, total_ref, *refs = refs
    if not first:
        old_out_ref, old_ref, *refs = refs
    if last:
        (out_ref,) = refs
    else:
        out_ref, sums_ref = refs
    starts = starts_ref[...]
    cosine, sine = cos_ref[...], sin_ref[...]

    def unrotate(part, cosine, sine):
        one, two = part[:HALF], part[HALF:ROT]
        return jnp.concatenate(
            [one * cosine + two * sine, two * cosine - one * sine, part[ROT:]], axis=0
        )

    def at_position(position):
        return pl.ds(pl.multiple_of(position * block, block), block)

    if last:
        for position in range(blocks):
            columns = slice(position * block, (position + 1) * block)
            out_ref[0, :, columns] = old_out_ref[:, columns]

    for mine in range(blocks):

        @pl.when(where_ref[base] == mine)
        def _(mine=mine):
            for head in range(PAIR):
                rows = slice(head * HEAD, (head + 1) * HEAD)
                query = q_ref[0, rows, :]
                grad = grad_ref[rows, :]
                row_total = total_ref[head]
                kept = []
                offset = jnp.zeros((1, block), F32)
                for other in range(mine + 1):
                    columns = slice(other * block, (other + 1) * block)
                    raw = contract(k_ref[0, rows, columns], query, 0, 0)
                    masked = jnp.where(allowed(other, mine, block, starts), raw, MASKED)
                    weights = jnp.exp(masked - row_total)
                    back = contract(v_ref[0, rows, columns], grad, 0, 0)
                    offset = offset + jnp.sum(weights * back, axis=0, keepdims=True)
                    kept.append((weights, back))
                query_sum = jnp.zeros((HEAD, block), F32)
                for other in range(blocks):
                    columns = slice(other * block, (other + 1) * block)
                    if other <= mine:
                        weights, back = kept[other]
                        change = (weights * (back - offset)).astype(BF16)
                        query_sum = query_sum + contract(k_ref[0, rows, columns], change, 1, 0)
                        key_sum = contract(query, change, 1, 1)
                        value_sum = contract(grad, weights.astype(BF16), 1, 1)
                        if not first:
                            key_sum = key_sum + old_ref[0, rows, columns]
                            value_sum = value_sum + old_ref[1, rows, columns]
                    elif first:
                        key_sum = jnp.zeros((HEAD, block), F32)
                        value_sum = jnp.zeros((HEAD, block), F32)
                    else:
                        key_sum = old_ref[0, rows, columns]
                        value_sum = old_ref[1, rows, columns]
                    if last:
                        there = at_position(lax.rem(where_ref[base + 2] + blocks - other, blocks))
                        turned = unrotate(
                            key_sum, all_cos_ref[:, columns], all_sin_ref[:, columns]
                        )
                        out_ref[1, rows, there] = turned.astype(BF16)
                        out_ref[2, rows, there] = value_sum.astype(BF16)
                    else:
                        sums_ref[0, rows, columns] = key_sum
                        sums_ref[1, rows, columns] = value_sum
                query_sum = unrotate(query_sum * (HEAD**-0.5), cosine, sine).astype(BF16)
                if last:
                    out_ref[0, rows, at_position(where_ref[base + 1])] = query_sum
                else:
                    out_ref[rows, :] = query_sum


def attend_back_block(where, base, starts, cosine, sine, buffer, grad, totals, before, last):
    _, width, length = buffer.shape
    block = grad.shape[1]
    rows = PAIR * HEAD
    heads, blocks = width // HEAD, length // block
    groups = width // rows
    first = before is None
    whole_table = pl.BlockSpec((HALF, length), lambda h, s: (0, 0))
    both = pl.BlockSpec((2, rows, length), lambda h, s: (0, h, 0))
    specs = [
        pl.BlockSpec((1, block), lambda h, s: (0, s[base])),
        pl.BlockSpec((HALF, block), lambda h, s: (0, s[base])),
        pl.BlockSpec((HALF, block), lambda h, s: (0, s[base])),
    ]
    args = [where, starts, cosine, sine]
    if last:
        specs += [whole_table, whole_table]
        args += [cosine, sine]
    specs += [
        pl.BlockSpec((1, rows, block), lambda h, s: (0, h, s[base])),
        pl.BlockSpec((1, rows, length), lambda h, s: (1, h, 0)),
        pl.BlockSpec((1, rows, length), lambda h, s: (2, h, 0)),
        pl.BlockSpec((rows, block), lambda h, s: (h, 0)),
        pl.BlockSpec((PAIR, 1, block), lambda h, s: (s[base + 3] * groups + h, 0, 0)),
    ]
    args += [buffer, buffer, buffer, grad, totals]
    aliases = {}
    if not first:
        if last:
            specs += [pl.BlockSpec((rows, length), lambda h, s: (h, 0)), both]
        else:
            specs += [pl.BlockSpec(memory_space=pl.ANY), both]
            aliases = {len(args): 0, len(args) + 1: 1}
        args += before
    if last:
        out_shape = jax.ShapeDtypeStruct((3, width, length), BF16)
        out_specs = pl.BlockSpec((3, rows, length), lambda h, s: (0, h, 0))
    else:
        out_shape = (
            jax.ShapeDtypeStruct((width, length), BF16),
            jax.ShapeDtypeStruct((2, width, length), F32),
        )
        out_specs = (pl.BlockSpec((rows, block), lambda h, s: (h, s[base + 1])), both)
    return pl.pallas_call(
        functools.partial(attend_back_kernel, blocks, block, base, first, last),
        out_shape=out_shape,
        grid_spec=pltpu.PrefetchScalarGridSpec(
            num_scalar_prefetch=1, grid=(groups,), in_specs=specs, out_specs=out_specs
        ),
        input_output_aliases=aliases,
        cost_estimate=pl.CostEstimate(
            flops=40 * width * block * length,
            bytes_accessed=2 * width * (10 * length + 3 * block),
            transcendentals=heads * block * length,
        ),
        name="attend_back_block",
    )(*args)


def per_device(
    ring_size,
    data_size,
    layer_input,
    output_grad,
    segment_ids,
    norm_gain,
    gain_mean,
    gain_square,
    norm_shift,
    shift_mean,
    shift_square,
    qkv_bias,
    bias_mean,
    bias_square,
    qkv_weight,
    qkv_mean,
    qkv_square,
    proj_weight,
    proj_mean,
    proj_square,
    feed_weight,
    feed_mean,
    feed_square,
    down_weight,
    down_mean,
    down_square,
):
    n = ring_size
    block, depth = layer_input.shape
    length = n * block
    width = qkv_bias.shape[1]
    units = feed_weight.shape[2]
    place = lax.axis_index("tensor")
    ring = [(i, (i + 1) % n) for i in range(n)]

    def after(value, *others):
        return lax.optimization_barrier((value, *others))[0]

    def pass_on(values, pairs=ring):
        return lax.ppermute(values, "tensor", pairs)

    def pass_up(values, first, last):
        return pass_on(values, [(i, i + 1) for i in range(first, last + 1)])

    def pass_down(values, first, last):
        return pass_on(values, [(i, i - 1) for i in range(first, last + 1)])

    def plus(term, moving):
        return (term + moving.astype(F32)).astype(BF16)

    arrivals = [
        sorted(
            [(d, 0) for d in range(1, z + 1)] + [(d, 1) for d in range(1, n - z)]
        )
        for z in range(n)
    ]

    taken = [
        sorted(range(1, n), key=lambda p: (p - 1 if p > z else n - 1 - p, p)) + [0]
        for z in range(n)
    ]

    def where_row(z):
        blocks = [(z - p) % n for p in range(n)] + [(z - p) % n for p in taken[z]]
        blocks += [z] + [z + d if above else z - d for d, above in arrivals[z]]
        return [
            v for b in blocks for v in (b, (z - b) % n, z, taken[z].index((z - b) % n))
        ]

    where = jnp.asarray([where_row(z) for z in range(n)], jnp.int32)[place]

    def choose(values, ranks):
        groups = sorted(set(ranks.values()))
        result = values[groups[0]]
        for rank in groups[1:]:
            here = functools.reduce(
                jnp.logical_or, [place == z for z, r in ranks.items() if r == rank]
            )
            result = jnp.where(here, values[rank], result)
        return result

    def gather_weight(shard, axis):
        return lax.all_gather(shard.astype(BF16), "dp", axis=axis, tiled=True)

    def apart(*values):
        return lax.optimization_barrier(values)

    inputs = layer_input.astype(F32)
    w_qkv = gather_weight(qkv_weight.transpose(0, 2, 1), 2).reshape(3 * width, depth)
    w_proj = gather_weight(proj_weight, 1)
    w_feed = gather_weight(feed_weight, 1)
    w_down = gather_weight(down_weight, 1)
    normed_one, unit_one, inverse_one = norm_forward(inputs, norm_gain[0], norm_shift[0])
    starts = run_starts(segment_ids)
    cosine, sine = rotary_tables(starts)
    (room,) = apart(jnp.zeros((4 * width, depth), BF16))
    rows_one = [normed_one.astype(BF16)]
    buffer = None
    for p in range(n):
        if p < n - 1:
            moved = pass_on(rows_one[p])
            rows_one.append(
                after(moved, cosine, sine, starts, where)
                if p == 0
                else moved
            )
        pre = contract(rows_one[p], w_qkv, 1, 1) + qkv_bias.reshape(1, 3 * width)
        buffer = rope_block(where, 4 * p, pre, cosine, sine, buffer, width, length)

    cotangent = after(output_grad, rows_one[n - 1])
    grad_up, grad_down_way = [cotangent], [cotangent]
    for hop in range(1, n):
        grad_up.append(pass_up(grad_up[hop - 1], hop - 1, n - 2))
        grad_down_way.append(pass_down(grad_down_way[hop - 1], 1, n - hop))

    mixed, totals, parts = [], [], []
    for rank in range(n):
        at = after(where, parts[-1]) if rank else where
        mixed_one, totals_one = attend_block(at, 4 * (n + rank), starts, buffer, block)
        mixed.append(mixed_one)
        totals.append(totals_one)
        term = contract(mixed_one, w_proj, 0, 0)
        parts.append(apart(term.astype(BF16) if rank < n - 1 else term)[0])

    def scatter_chains(parts, rank_of, gate=()):
        first = choose(parts, {0: rank_of(0, 1), n - 1: rank_of(n - 1, n - 1)})
        up = down = pass_on(after(first, *gate), [(0, 1), (n - 1, n - 2)])
        for step in range(1, n - 1):
            up_ranks = {z: rank_of(z, step + 1) for z in range(step + 1)}
            down_ranks = {z: rank_of(z, n - 1 - step) for z in range(n - 1 - step, n)}
            ready = up if step == 1 else after(up, send_down)
            send_up = plus(choose(parts, up_ranks).astype(F32), ready)
            send_down = plus(
                choose(parts, down_ranks).astype(F32), after(down, send_up)
            )
            up = pass_up(send_up, 0, step)
            down = pass_down(send_down, n - 1 - step, n - 1)
        return parts[rank_of(0, 0)].astype(F32) + up.astype(F32) + down.astype(F32)

    middle = inputs + scatter_chains(parts, lambda z, p: taken[z].index(p))
    grad_rows = [output_grad] + [
        jnp.where(place >= p, grad_up[p], grad_down_way[n - p]) for p in range(1, n)
    ]

    normed_two, unit_two, inverse_two = norm_forward(middle, norm_gain[1], norm_shift[1])
    rows_two = [normed_two.astype(BF16)]
    for hop in range(1, n):
        rows_two.append(pass_on(rows_two[hop - 1]))
    halves = [range(n // 2), range(n // 2, n)]
    rows_half, grad_half, hidden, gate_grads, upper_grads = [], [], [], [], []
    out_parts, back_parts = [], []
    for half in halves:
        rows_here, grads_here = apart(
            jnp.concatenate([rows_two[p] for p in half], axis=0),
            jnp.concatenate([grad_rows[p] for p in half], axis=0),
        )
        rows_half.append(rows_here)
        grad_half.append(grads_here)
        gate = jnp.dot(rows_here, w_feed[0], preferred_element_type=F32)
        upper = jnp.dot(rows_here, w_feed[1], preferred_element_type=F32)
        grad_hidden = contract(grads_here, w_down, 1, 1)
        sigma = jax.nn.sigmoid(gate)
        swish = gate * sigma
        hidden_low = (swish * upper).astype(BF16)
        gate_low = (grad_hidden * upper * sigma * (1.0 + gate * (1.0 - sigma))).astype(BF16)
        upper_low = (grad_hidden * swish).astype(BF16)
        hidden_low, gate_low, upper_low = apart(hidden_low, gate_low, upper_low)
        hidden.append(hidden_low)
        gate_grads.append(gate_low)
        upper_grads.append(upper_low)
        term = contract(gate_low, w_feed[0], 1, 1) + contract(upper_low, w_feed[1], 1, 1)
        (term,) = apart(term.astype(BF16))
        back_parts.extend(jnp.split(term, len(half), axis=0))
        (term,) = apart(jnp.dot(hidden_low, w_down, preferred_element_type=F32).astype(BF16))
        out_parts.extend(jnp.split(term, len(half), axis=0))

    def scatter_sum(grad, axis):
        return lax.psum_scatter(grad, "dp", scatter_dimension=axis, tiled=True)

    grad_down = contract(
        jnp.concatenate(hidden, axis=0), jnp.concatenate(grad_half, axis=0), 0, 0
    ).astype(BF16)
    down_sum = scatter_sum(grad_down, 1).astype(F32)
    (all_gates,) = apart(jnp.concatenate(gate_grads + upper_grads, axis=0))
    grad_feed = jnp.einsum(
        "krf,rd->kfd",
        all_gates.reshape(2, length, units),
        jnp.concatenate(rows_half, axis=0),
        preferred_element_type=F32,
    ).astype(BF16)
    feed_sum = with_layout_constraint(
        scatter_sum(grad_feed, 2).transpose(0, 2, 1), Layout((0, 1, 2))
    ).astype(F32)

    moving = None
    for step in range(1, n):
        if moving is None:
            send = after(back_parts[step], rows_two[n - 1])
        else:
            send = plus(back_parts[step].astype(F32), moving)
        moving = pass_on(send)
    grad_normed_two = back_parts[0].astype(F32) + moving.astype(F32)

    grad_middle = output_grad.astype(F32) + norm_backward(
        grad_normed_two, unit_two, inverse_two, norm_gain[1]
    )
    gain_two = jnp.sum(grad_normed_two * unit_two, axis=0)
    shift_two = jnp.sum(grad_normed_two, axis=0)

    own = grad_middle.astype(BF16)
    ups, downs = [own], [own]
    all_totals = jnp.concatenate(totals, axis=0)
    slots, before = [own], None

    def back_block(slot, last):
        grad_mixed = contract(w_proj, slots[slot], 1, 1).astype(BF16)
        return attend_back_block(
            where,
            4 * (2 * n + slot),
            starts,
            cosine,
            sine,
            buffer,
            grad_mixed,
            all_totals,
            before,
            last,
        )

    for hop in range(1, n):
        ups.append(pass_up(ups[hop - 1], hop - 1, n - 2))
        downs.append(pass_down(downs[hop - 1], 1, n - hop))
        before = back_block(hop - 1, False)
        chosen, here = None, after(place, slots[hop - 1])
        for z in range(n):
            d, above = arrivals[z][hop - 1]
            value = downs[d] if above else ups[d]
            chosen = value if chosen is None else jnp.where(here == z, value, chosen)
        slots.append(apart(chosen)[0])
    grad_pre = back_block(n - 1, True)
    layer_output = middle + scatter_chains(out_parts, lambda z, p: p, (ups[1], downs[1]))

    flat_pre = grad_pre.reshape(3 * width, length)
    moving, first_parts = None, [None] * n
    for step in [*range(1, n), 0]:
        term = contract(flat_pre[:, step * block : (step + 1) * block], w_qkv, 0, 0)
        first_parts[step] = apart(term.astype(BF16) if step == 1 else term)[0]
    for step in range(1, n):
        send = first_parts[1] if moving is None else plus(first_parts[step], moving)
        moving = pass_on(send)
    grad_normed_one = first_parts[0] + moving.astype(F32)
    grad_qkv = contract(flat_pre, jnp.concatenate(rows_one, axis=0), 1, 0).astype(BF16)
    all_mixed = jnp.concatenate(mixed, axis=1)
    mixed_slots = [
        lax.dynamic_slice_in_dim(all_mixed, where[4 * (2 * n + slot) + 3] * block, block, 1)
        for slot in range(n)
    ]
    grad_proj = contract(
        jnp.concatenate(mixed_slots, axis=1), jnp.concatenate(slots, axis=0), 1, 0
    ).astype(BF16)
    grad_both = lax.dynamic_update_slice(room, grad_proj, (3 * width, 0))
    grad_both = lax.dynamic_update_slice(grad_both, grad_qkv, (0, 0))
    both_rows = scatter_sum(grad_both, 1).astype(F32)
    qkv_sum = both_rows[: 3 * width].reshape(3, width, depth // data_size).transpose(0, 2, 1)
    proj_sum = both_rows[3 * width :]

    bias_local = jnp.sum(grad_pre.astype(F32), axis=2)
    input_grad = grad_middle + norm_backward(grad_normed_one, unit_one, inverse_one, norm_gain[0])
    gain_one = jnp.sum(grad_normed_one * unit_one, axis=0)
    shift_one = jnp.sum(grad_normed_one, axis=0)

    def sum_over(values, axis, size):
        step = 1
        while step < size:
            other = lax.ppermute(values, axis, [(i, i ^ step) for i in range(size)])
            values = values + other
            step *= 2
        return values

    small = jnp.concatenate(
        [gain_one, gain_two, shift_one, shift_two, bias_local.reshape(3 * width)]
    )
    small = sum_over(small.reshape(-1, 128), "dp", data_size).reshape(-1)
    bias_grad = small[4 * depth :].reshape(3, width)
    small = sum_over(small[: 4 * depth].reshape(-1, 128), "tensor", n)
    gain_total, shift_total = small.reshape(2, 2, depth)

    outputs = [layer_output, input_grad]
    groups = (
        (norm_gain, gain_total, gain_mean, gain_square),
        (norm_shift, shift_total, shift_mean, shift_square),
        (qkv_bias, bias_grad, bias_mean, bias_square),
        (qkv_weight, qkv_sum, qkv_mean, qkv_square),
        (proj_weight, proj_sum, proj_mean, proj_square),
        (feed_weight, feed_sum, feed_mean, feed_square),
        (down_weight, down_sum, down_mean, down_square),
    )
    for which, (param_arr, grad_total, mean_in, square_in) in enumerate(groups):
        change, mean_new, square_new = adamw(param_arr, grad_total, mean_in, square_in)
        shown = change if which < 3 else param_arr + change
        outputs.extend([grad_total, shown, mean_new, square_new])
    return tuple(outputs)


def solution(mesh):
    tokens, small, bias = P(("dp", "tensor"), None), P(), P(None, "tensor")
    three, two = P(None, "dp", "tensor"), P("tensor", "dp")
    per_param = [small] * 6 + [bias] * 3 + [three] * 3 + [two] * 3 + [three] * 3 + [two] * 3
    outs = [small] * 8 + [bias] * 4 + [three] * 4 + [two] * 4 + [three] * 4 + [two] * 4
    n = mesh.shape["tensor"]

    def body(*args):
        return per_device(n, mesh.shape["dp"], *args)

    return jax.shard_map(
        body,
        mesh=mesh,
        in_specs=(tokens, tokens, P("dp", None), *per_param),
        out_specs=(tokens, tokens, *outs),
        check_vma=False,
    )
```
